256 devices in a mesh: seq: 32 (over x, z), mp: 8 (over y, core).
Axes of the slice: x: 4, y: 4, z: 8, core: 2. Of those that a mesh axis runs over, the one named last changes fastest.
Arguments:
- hidden_in: bfloat16 [64, 2048], P('mp'), may hold values from -24 to 24
- query_weight: bfloat16 [2048, 3072], P(None, 'seq'), may hold values from -0.25 to 0.25
- key_absorb: bfloat16 [16, 128, 512], replicated, may hold values from -0.5 to 0.5
- value_up: bfloat16 [16, 512, 128], replicated, may hold values from -0.25 to 0.25
- out_weight: bfloat16 [2048, 2048], P(None, 'seq'), may hold values from -0.5 to 0.5
- latent_cache: bfloat16 [64, 4096, 576], P('mp', 'seq'), may hold values from -41 to 41
- cache_lengths: int32 [64], P('mp'), may hold values from 128 to 4096, as said below
- keep_lists: int32 [64, 32, 64], P('mp', 'seq'), may hold values from 0 to 127, as said below
- drop_weights: int32 [64, 4096], P('mp', 'seq'), may hold values from 1 to 8
- pack_dest: int32 [64, 32], P('mp'), may hold values from -1 to 127, as said below
- final_gain: bfloat16 [2048], replicated, may hold values from 0.5 to 1.5
- head_weight: bfloat16 [2048, 102400], P(None, ('seq', 'mp')), may hold values from -0.125 to 0.125
- tenant_ranges: int32 [4, 2], replicated, may hold values from 0 to 102400, as said below
- tenant_ids: int32 [64], replicated, may hold values from 0 to 3
Outputs:
- packed_rows: bfloat16 [1024, 64, 576], P(('seq', 'mp'))
- packed_summary: bfloat16 [1024, 576], P(('seq', 'mp'))
- hidden_out: bfloat16 [64, 2048], P('mp', 'seq')
- state_norm: float32 [64], P('mp')
- top_logit: float32 [64], P('mp')
The draws below stay inside these ranges and needn't reach their ends.
Inputs may be any that keep to these rules, and one draw needn't show every extreme that they name: `cache_lengths`: every length is a whole number of 128-position blocks, at least one block. Within each group of 8 requests (one index of mp) the lengths add up to 16384, and some request of the group has the full 4096. `keep_lists`: the 64 positions of a block are distinct and ascending. pack_dest[r, b] is -1 exactly when block b of request r is not live; otherwise it is owner * 4 + slot with an owner in 0 to 32 - 1 (an index of seq) and a slot in 0 to 3. Within one group of 8 requests the live blocks take every destination exactly once. Of the live blocks of one block index in one group, at most 1 go to any one owner, and those that share an owner take consecutive slots. Block index 0 is live for every request of a group, and some owner receives 1 of them. `tenant_ranges`: row t is tenant t's window [low, high) of vocabulary entries; each window holds at least 51200 entries.
All inputs are finite; a program needn't handle non-finite values.
Results may differ from the reference program's by a relative error of at most 0.0075.
Values may be sent and summed in bfloat16 or wider, within the bound.
No kernel may reach another device: no remote copies, remote signals or barrier semaphores. Data moves between devices by JAX's collectives and lax.ppermute only.
A program may use at most 128 MiB of HBM per device.

```python
import jax
import jax.numpy as jnp
from jax import lax

D = 2048
H = 16
NOPE = 128
ROPE = 64
LAT = 512
VH = 128
V = 102400
BLK = 128
KB = 64
TENANTS = 4
RQ = 8
R = 64
NB = 32
MAXLEN = 4096
SLOTS = 4
POOL = 1024
N_MP = 8


def block_counts(key):
    half_blocks = NB // 2

    def one_group(group_key):
        spread_key, order_key = jax.random.split(group_key)
        spread_draw = jax.random.randint(spread_key, (RQ // 2 - 2,), -(half_blocks - 1), half_blocks)
        paired = jnp.stack([half_blocks + spread_draw, half_blocks - spread_draw], axis=1).reshape(-1)
        leading = jnp.array([NB, 1, half_blocks - 1, half_blocks], dtype=jnp.int32)
        counts = jnp.concatenate([leading, paired.astype(jnp.int32)])
        return counts[jax.random.permutation(order_key, RQ)]
    return jax.vmap(one_group)(jax.random.split(key, R // RQ))


def draw_cache_lengths(key, part):
    return (block_counts(jax.random.fold_in(key, 11)) * BLK).reshape(R).astype(jnp.int32)


def draw_pack_dest(key, part):
    counts = block_counts(jax.random.fold_in(key, 11))
    slot_count = RQ // 2

    def one_group(counts_row, group_key):
        order_key, owner_key = jax.random.split(group_key)
        priority = jnp.argsort(jax.random.permutation(order_key, RQ)).astype(jnp.int32)
        live_mask = (jnp.arange(NB, dtype=jnp.int32)[None, :] < counts_row[:, None]).astype(jnp.int32)
        per_source = jnp.sum(live_mask, axis=0)
        offsets = jnp.cumsum(per_source) - per_source
        before = (priority[None, :] < priority[:, None]).astype(jnp.int32)
        within = jnp.matmul(before, live_mask)
        order_rank = offsets[None, :] + within
        owners = jax.random.permutation(owner_key, NB).astype(jnp.int32)
        destination = owners[order_rank % NB] * slot_count + order_rank // NB
        return jnp.where(live_mask > 0, destination, -1)
    group_keys = jax.random.split(jax.random.fold_in(key, 23), R // RQ)
    return jax.vmap(one_group)(counts, group_keys).reshape(R, NB).astype(jnp.int32)


def draw_keep_lists(key, part):
    scores = jax.random.randint(key, (R, NB, BLK), 0, 1 << 20) * BLK + jnp.arange(BLK, dtype=jnp.int32)
    chosen = jnp.argsort(scores, axis=-1)[..., :KB]
    return jnp.sort(chosen, axis=-1).astype(jnp.int32)


def draw_tenant_ranges(key, part):
    low_key, span_key = jax.random.split(key)
    tenant_index = jnp.arange(TENANTS, dtype=jnp.int32)
    window_low = jax.random.randint(low_key, (TENANTS,), 0, V // 4 + 1)
    window_low = jnp.where(tenant_index == 0, 0, window_low)
    window_span = jax.random.randint(span_key, (TENANTS,), V // 2, 3 * V // 4 + 1)
    window_high = jnp.where(tenant_index == 1, V, window_low + window_span)
    return jnp.stack([window_low, window_high], axis=1).astype(jnp.int32)


def draw_hidden_in(key, part):
    value_key, offset_key = jax.random.split(jax.random.fold_in(key, 5))
    base = jnp.clip(jax.random.normal(value_key, (R, D), jnp.float32), -6.0, 6.0) * 0.5
    offset = jax.random.randint(offset_key, (), 0, NB)
    heavy_block = (jnp.arange(R, dtype=jnp.int32) + offset) % NB
    column_block = jnp.arange(D, dtype=jnp.int32) // (D // NB)
    factor = jnp.where(column_block[None, :] == heavy_block[:, None], 8.0, 1.0)
    return (base * factor).astype(jnp.bfloat16)


def draw_latent_cache(key, part):
    shape_full = (R, MAXLEN, LAT + ROPE)
    value_key = jax.random.fold_in(key, 0)
    sign_key = jax.random.fold_in(key, 2)
    level_key = jax.random.fold_in(key, 3)
    values_base = jnp.clip(jax.random.normal(value_key, shape_full, jnp.float32), -6.0, 6.0)
    pattern = jnp.where(jax.random.randint(sign_key, (1, 1, LAT + ROPE), 0, 2) == 0, -1.0, 1.0)
    spiked = jax.random.randint(level_key, (R, MAXLEN, 1), 0, 64)
    level = jnp.where(spiked == 0, 41.0, 38.0)
    return jnp.where(spiked < 2, level * pattern, values_base).astype(jnp.bfloat16)


def with_ends(entries, rng, least, largest):
    longest = entries.shape.index(max(entries.shape))
    spots = []
    for shift in (0, 1):
        where = [jax.random.randint(jax.random.fold_in(rng, axis), (), 0, length) for axis, length in enumerate(entries.shape)]
        where[longest] = (where[longest] + shift) % entries.shape[longest]
        spots.append(tuple(where))
    return entries.at[spots[0]].set(least).at[spots[1]].set(largest)


def levels(key, extent, shards, smallest, high):
    loudness = 1.0
    for position, blocks in shards:
        steps = jax.random.uniform(jax.random.fold_in(jax.random.fold_in(key, 6), position), (blocks,), jnp.float32, smallest / len(shards), high / len(shards))
        loudness = loudness * jnp.repeat(jnp.exp(steps), extent[position] // blocks).reshape((-1,) + (1,) * (len(extent) - 1 - position))
    return loudness


def scatter_about(own_key, shape, scale, most, cuts=(), kind=jnp.bfloat16):
    drawn = scale * jax.random.normal(own_key, shape, jnp.float32)
    if cuts:
        drawn = drawn * levels(own_key, shape, cuts, -0.22, 0.18)
    return jnp.clip(drawn, -most, most).astype(kind)


def setup_inputs(seed: int = 0) -> dict:
    key_of = jax.random.split(jax.random.key(seed), 15)
    return {
        "hidden_in": draw_hidden_in(jax.random.fold_in(key_of[14], 71), 0),
        "query_weight": scatter_about(key_of[1], (D, H * (NOPE + ROPE)), (D // 4) ** -0.5, 0.25, ((1, 32),)),
        "key_absorb": scatter_about(key_of[2], (H, NOPE, LAT), NOPE ** -0.5, 0.5),
        "value_up": scatter_about(key_of[3], (H, LAT, VH), LAT ** -0.5, 0.25),
        "out_weight": scatter_about(key_of[4], (H * VH, D), (H * VH // 16) ** -0.5, 0.5, ((1, 32),)),
        "latent_cache": draw_latent_cache(jax.random.fold_in(key_of[14], 71), 0),
        "cache_lengths": draw_cache_lengths(jax.random.fold_in(key_of[14], 71), 0),
        "keep_lists": draw_keep_lists(jax.random.fold_in(key_of[14], 71), 0),
        "drop_weights": with_ends(jax.random.randint(key_of[8], (R, MAXLEN), 1, 9), jax.random.fold_in(key_of[8], 1), 1, 8).astype(jnp.int32),
        "pack_dest": draw_pack_dest(jax.random.fold_in(key_of[14], 71), 0),
        "final_gain": jnp.clip(1.0 + 0.1 * jax.random.normal(key_of[10], (D,), jnp.float32), 0.5, 1.5).astype(jnp.bfloat16),
        "head_weight": scatter_about(key_of[11], (D, V), D ** -0.5, 0.125, ((1, 256),)),
        "tenant_ranges": draw_tenant_ranges(jax.random.fold_in(key_of[14], 71), 0),
        "tenant_ids": with_ends(jax.random.randint(key_of[13], (R,), 0, TENANTS), jax.random.fold_in(key_of[13], 1), 0, TENANTS - 1).astype(jnp.int32),
    }


NEGATIVE = -1e+30
HIGHEST = lax.Precision.HIGHEST

def compact_request(cache_rows, keep_rows, weight_rows):
    blocks = cache_rows.reshape(NB, BLK, LAT + ROPE)
    kept_rows = jnp.take_along_axis(blocks, keep_rows[:, :, None], axis=1)
    positions = jnp.arange(BLK, dtype=jnp.int32)
    kept_flag = lax.optimization_barrier(jnp.sum((keep_rows[:, :, None] == positions[None, None, :]).astype(jnp.float32), axis=1))
    weights_dropped = weight_rows.reshape(NB, BLK).astype(jnp.float32) * (1.0 - kept_flag)
    weight_mass = lax.optimization_barrier(jnp.sum(weights_dropped, axis=1))
    summed = jnp.einsum('bt,btc->bc', weights_dropped, blocks.astype(jnp.float32), precision=HIGHEST)
    summary = (summed / weight_mass[:, None]).astype(jnp.bfloat16)
    return (kept_rows, summary)

def attend_request(query_lat, query_rope, kept_rows, summary, live_blocks):
    score_scale = (NOPE + ROPE) ** (-0.5)
    key_lat = kept_rows[:, :, :LAT].astype(jnp.float32)
    key_rope = kept_rows[:, :, LAT:].astype(jnp.float32)
    lat_query = query_lat.astype(jnp.float32)
    rope_query = query_rope.astype(jnp.float32)
    summary_f = summary.astype(jnp.float32)
    row_scores = (jnp.einsum('hl,bkl->hbk', lat_query, key_lat, precision=HIGHEST) + jnp.einsum('hr,bkr->hbk', rope_query, key_rope, precision=HIGHEST)) * score_scale
    summ_scores = (jnp.einsum('hl,bl->hb', lat_query, summary_f[:, :LAT], precision=HIGHEST) + jnp.einsum('hr,br->hb', rope_query, summary_f[:, LAT:], precision=HIGHEST)) * score_scale
    summ_scores = summ_scores + jnp.log(jnp.float32(BLK - KB))
    row_scores = jnp.where(live_blocks[None, :, None], row_scores, NEGATIVE)
    summ_scores = jnp.where(live_blocks[None, :], summ_scores, NEGATIVE)
    maxima = jnp.maximum(lax.optimization_barrier(jnp.max(row_scores, axis=(1, 2))), lax.optimization_barrier(jnp.max(summ_scores, axis=1)))
    row_weights = jnp.where(live_blocks[None, :, None], jnp.exp(row_scores - maxima[:, None, None]), 0.0)
    summ_weights = jnp.where(live_blocks[None, :], jnp.exp(summ_scores - maxima[:, None]), 0.0)
    totals = lax.optimization_barrier(jnp.sum(row_weights, axis=(1, 2))) + lax.optimization_barrier(jnp.sum(summ_weights, axis=1))
    weighted = jnp.einsum('hbk,bkl->hl', row_weights, key_lat, precision=HIGHEST) + jnp.einsum('hb,bl->hl', summ_weights, summary_f[:, :LAT], precision=HIGHEST)
    return (weighted / totals[:, None]).astype(jnp.bfloat16)

def reference(hidden_in, query_weight, key_absorb, value_up, out_weight, latent_cache, cache_lengths, keep_lists, drop_weights, pack_dest, final_gain, head_weight, tenant_ranges, tenant_ids):
    query_full = jnp.dot(hidden_in, query_weight, preferred_element_type=jnp.float32).astype(jnp.bfloat16)
    query_full = query_full.reshape(R, H, NOPE + ROPE)
    query_nope = query_full[:, :, :NOPE]
    query_rope = query_full[:, :, NOPE:]
    query_latent = jnp.einsum('rhn,hnl->rhl', query_nope.astype(jnp.float32), key_absorb.astype(jnp.float32), precision=HIGHEST).astype(jnp.bfloat16)

    def per_request(inputs):
        cache_rows, keep_rows, weight_rows, length_row, lat_row, rope_row = inputs
        kept_rows, summary = compact_request(cache_rows, keep_rows, weight_rows)
        live_blocks = jnp.arange(NB, dtype=jnp.int32) * BLK < length_row
        attended = attend_request(lat_row, rope_row, kept_rows, summary, live_blocks)
        return (kept_rows, summary, attended)
    kept_all, summary_all, attended = lax.map(per_request, (latent_cache, keep_lists, drop_weights, cache_lengths, query_latent, query_rope))
    group_index = (jnp.arange(R, dtype=jnp.int32) // RQ)[:, None]
    owner_index = pack_dest // SLOTS
    slot_index = pack_dest % SLOTS
    where_to = jnp.where(pack_dest >= 0, (owner_index * N_MP + group_index) * SLOTS + slot_index, POOL).astype(jnp.int32)
    packed_rows = jnp.zeros((POOL, KB, LAT + ROPE), jnp.bfloat16).at[where_to.reshape(-1)].set(kept_all.reshape(-1, KB, LAT + ROPE), mode='drop')
    packed_summary = jnp.zeros((POOL, LAT + ROPE), jnp.bfloat16).at[where_to.reshape(-1)].set(summary_all.reshape(-1, LAT + ROPE), mode='drop')
    values = jnp.einsum('rhl,hlv->rhv', attended.astype(jnp.float32), value_up.astype(jnp.float32), precision=HIGHEST)
    values = values.astype(jnp.bfloat16).reshape(R, H * VH)
    hidden_out = (hidden_in.astype(jnp.float32) + jnp.dot(values, out_weight, preferred_element_type=jnp.float32)).astype(jnp.bfloat16)
    rows_f = hidden_out.astype(jnp.float32)
    mean_sq = lax.optimization_barrier(jnp.mean(rows_f * rows_f, axis=1))
    state_norm = jnp.sqrt(mean_sq)
    normed = (rows_f * lax.rsqrt(mean_sq + 1e-06)[:, None] * final_gain.astype(jnp.float32)[None, :]).astype(jnp.bfloat16)
    logits = jnp.dot(normed, head_weight, preferred_element_type=jnp.float32)
    window_low = tenant_ranges[tenant_ids, 0]
    window_high = tenant_ranges[tenant_ids, 1]
    columns = jnp.arange(V, dtype=jnp.int32)
    allowed = (columns[None, :] >= window_low[:, None]) & (columns[None, :] < window_high[:, None])
    top_logit = lax.optimization_barrier(jnp.max(jnp.where(allowed, logits, NEGATIVE), axis=1))
    return (packed_rows, packed_summary, hidden_out, state_norm, top_logit)
```

```python
import functools

import jax
import jax.numpy as jnp
from jax import lax
from jax.experimental import pallas as pl
from jax.experimental.pallas import tpu as pltpu
from jax.sharding import Mesh, PartitionSpec as P

H = 16
NOPE = 128
ROPE = 64
LAT = 512
VH = 128
BLK = 128
KB = 64
TENANTS = 4
RQ = 8
ROW = LAT + ROPE
HALF = (NOPE + ROPE) // 2
WIDE = H * VH
SEQ = ("sx", "sz")
MP = ("y", "c")
ALL = SEQ + MP

NEGATIVE = -1e30
F32 = jnp.float32
BF16 = jnp.bfloat16
NT = (((1,), (1,)), ((), ()))


def mm(a, b):
    return jnp.dot(a, b, preferred_element_type=F32)


def mm_nt(a, b):
    return lax.dot_general(a, b, NT, preferred_element_type=F32)


def iota(shape, axis):
    return lax.broadcasted_iota(jnp.int32, shape, axis)


WHOLE = pl.BlockSpec(memory_space=pltpu.VMEM)
APART = pl.BlockSpec(memory_space=pltpu.HBM)
SCALAR = pl.BlockSpec(memory_space=pltpu.SMEM)


def vmem_call(kernel, out_shape, scratch=(), limit=16 << 20, **specs):
    return pl.pallas_call(
        kernel,
        out_shape=out_shape,
        scratch_shapes=list(scratch),
        **specs,
        compiler_params=pltpu.CompilerParams(vmem_limit_bytes=limit),
    )


def in_parts(x):
    high = x.astype(BF16).astype(F32)
    rest = x - high
    middle = rest.astype(BF16).astype(F32)
    return (high, middle, rest - middle)


def spread_kernel(cache_ref, keep_ref, message_ref, out_ref, sem):
    rows = out_ref.shape[0] * RQ
    lane = iota((rows, BLK), 1)
    request = iota((rows, BLK), 0) % RQ
    keys = keep_ref[...]
    none = jnp.zeros((ROPE, BLK), BF16)
    tail = jnp.zeros((rows, 2 * ROPE), F32)
    for k in range(2):
        kept = jnp.zeros((rows, LAT), F32)
        chosen = jnp.where(lane == keys[:, k : k + 1], request, -1)
        for r in range(RQ):
            onehot = (chosen == r).astype(F32).astype(BF16)
            kept = kept + mm_nt(onehot, cache_ref[r, :LAT, :])
            rope = cache_ref[r, LAT:, :]
            rope = jnp.concatenate([rope, none] if k == 0 else [none, rope], axis=0)
            tail = tail + mm_nt(onehot, rope)
        for c in range(LAT // 128):
            at = (2 * c + k) * RQ
            for i in range(out_ref.shape[0]):
                out_ref[i, at : at + RQ, :] = kept[
                    RQ * i : RQ * i + RQ, 128 * c : 128 * c + 128
                ].astype(BF16)
    for i in range(out_ref.shape[0]):
        out_ref[i, 64:72, :] = tail[RQ * i : RQ * i + RQ, :].astype(BF16)
    copy = pltpu.make_async_copy(out_ref, message_ref.at[:, RQ:, :], sem)
    copy.start()
    copy.wait()


def attend_kernel(
    query_ref,
    absorb_ref,
    cache_ref,
    summ_ref,
    summ_tail_ref,
    mask_ref,
    live_ref,
    summ_send_ref,
    out_ref,
    lat_ref,
    tail_ref,
    absorb_here,
    sems,
):
    copies = [
        pltpu.make_async_copy(absorb_ref.at[h], absorb_here.at[h], sems.at[h]) for h in range(H)
    ]
    for copy in copies:
        copy.start()
    for h in range(H):
        copies[h].wait()
        first = query_ref[2 * h].astype(F32)
        second = query_ref[2 * h + 1].astype(F32)
        nope = jnp.where(iota(first.shape, 1) < HALF, first, second).astype(BF16)
        lat_ref[8 * h : 8 * h + 8, :] = mm(nope, absorb_here[h])
        tail_ref[8 * h : 8 * h + 8, :] = second[:, :ROPE]
    lat = lat_ref[...].astype(BF16)
    tail = tail_ref[...].astype(BF16)
    rows = H * RQ
    request = iota((rows, BLK), 0) % RQ
    scores = jnp.zeros((rows, BLK), F32)
    for r in range(RQ):
        found = mm(lat, cache_ref[r, :LAT, :]) + mm(tail, cache_ref[r, LAT:, :])
        scores = jnp.where(request == r, found, scores)
    scale = (NOPE + ROPE) ** (-0.5)
    usable = jnp.concatenate([mask_ref[...]] * H, axis=0) > 0.0
    live = jnp.concatenate([live_ref[...]] * H, axis=0) > 0.0
    scores = jnp.where(usable, scores * scale, NEGATIVE)
    summ_all = mm_nt(lat, summ_ref[...]) + mm_nt(tail, summ_tail_ref[...])
    own = iota((rows, RQ), 1) == iota((rows, RQ), 0) % RQ
    summ = jnp.sum(jnp.where(own, summ_all, 0.0), axis=1, keepdims=True)
    summ = summ * scale + jnp.log(F32(BLK - KB))
    live_col = live[:, :1]
    summ = jnp.where(live_col, summ, NEGATIVE)
    top = jnp.maximum(jnp.max(scores, axis=1, keepdims=True), summ)
    weights = jnp.where(usable, jnp.exp(scores - top), 0.0)
    summ_weight = jnp.where(live_col, jnp.exp(summ - top), 0.0)
    total = jnp.sum(weights, axis=1, keepdims=True) + summ_weight
    summ_spread = jnp.where(own, summ_weight, 0.0)
    high = weights.astype(BF16)
    low = (weights - high.astype(F32)).astype(BF16)
    summ_high = summ_spread.astype(BF16)
    summ_low = (summ_spread - summ_high.astype(F32)).astype(BF16)
    weighted = mm(summ_high, summ_ref[...]) + mm(summ_low, summ_ref[...])
    none = jnp.zeros((rows, BLK), BF16)
    for r in range(RQ):
        keys = cache_ref[r, :LAT, :]
        weighted = weighted + mm_nt(jnp.where(request == r, high, none), keys)
        weighted = weighted + mm_nt(jnp.where(request == r, low, none), keys)

    def halves(first, second):
        upper = iota(first.shape, 0) % RQ < RQ // 2
        return (
            jnp.where(upper, first, pltpu.roll(second, RQ // 2, 0)),
            jnp.where(upper, pltpu.roll(first, rows - RQ // 2, 0), second),
        )

    large = weighted.astype(BF16).astype(F32)
    sent = halves(large, weighted - large)
    lane = iota((rows, 128), 1)
    side = jnp.zeros((rows, 128), F32)
    for at, column in enumerate(in_parts(top) + in_parts(total)):
        side = jnp.where(lane == 96 + at, column, side)
    sides = halves(side, side)
    for h in range(H):
        cut = slice(RQ * h, RQ * h + RQ)
        for half in range(2):
            d = 2 * h + half
            for c in range(LAT // 128):
                out_ref[d, RQ * c : RQ * c + RQ, :] = sent[half][
                    cut, 128 * c : 128 * c + 128
                ].astype(BF16)
            out_ref[d, 32:40, :] = (sides[half][cut] + summ_send_ref[d].astype(F32)).astype(BF16)


def merge_kernel(head_ref, parts_ref, up_ref, half_ref, before_ref, message_ref, out_ref, up_here, sems):
    fetch = pltpu.make_async_copy(up_ref.at[head_ref[0]], up_here, sems.at[0])
    fetch.start()
    count = parts_ref.shape[0]
    sides = []
    for i in range(count):
        side = parts_ref[i, 32:40, :].astype(F32)
        sides.append(side + pltpu.roll(side, 127, 1) + pltpu.roll(side, 126, 1))
    lane = iota((RQ, 128), 1)
    sides = [jnp.where((lane == 96) | (lane == 99), one, 0.0) for one in sides]
    top = functools.reduce(jnp.maximum, [one[:, 96:97] for one in sides])
    factors = [jnp.exp(one[:, 96:97] - top) for one in sides]
    total = functools.reduce(jnp.add, [f * one[:, 99:100] for f, one in zip(factors, sides)])
    attended = []
    for c in range(LAT // 128):
        column = jnp.zeros((RQ, 128), F32)
        for i in range(count):
            block = parts_ref[i, RQ * c : RQ * c + RQ, :].astype(F32)
            column = column + factors[i] * block
        column = column + pltpu.roll(column, RQ // 2, 0)
        attended.append((column / total).astype(BF16))
    fetch.wait()
    values = mm(jnp.concatenate(attended, axis=1), up_here[...])
    values = jnp.where(half_ref[...] > 0.0, values, 0.0).astype(BF16)
    for d in range(out_ref.shape[0]):
        out_ref[d] = values
    copy = pltpu.make_async_copy(out_ref, message_ref.at[:, :RQ, :], sems.at[1])
    copy.start()
    copy.wait()


def hidden_kernel(parts_ref, weight_ref, residual_ref, side_ref, dest_ref, out_ref, own_ref):
    count = parts_ref.shape[0]
    values = [
        (parts_ref[2 * h, :RQ, :].astype(F32) + parts_ref[2 * h + 1, :RQ, :].astype(F32)).astype(BF16)
        for h in range(H)
    ]
    total = mm_nt(jnp.concatenate(values, axis=1), weight_ref[...])
    total = residual_ref[...].astype(F32) + total
    own_ref[...] = total.astype(BF16)
    both = jnp.where(side_ref[...] > 0.0, total, 0.0).astype(BF16)
    for d in range(count):
        out_ref[d, :RQ, :] = both
    rows = count * RQ
    row = iota((rows, rows), 0)
    matches = dest_ref[...] == row // RQ * (RQ // 2) + row % (RQ // 2)
    upper = row % RQ < RQ // 2
    first = (matches & upper).astype(F32).astype(BF16)
    second = (matches & ~upper).astype(F32).astype(BF16)

    def group(g):
        return parts_ref[:, RQ + RQ * g : 2 * RQ + RQ * g, :].reshape(rows, 128)

    for q in range(5):
        picked = mm(first, group(2 * q))
        if q < 4:
            picked = picked + mm(second, group(2 * q + 1))
        out_ref[:, RQ + RQ * q : 2 * RQ + RQ * q, :] = picked.astype(BF16).reshape(count, RQ, 128)


def settle_kernel(parts_ref, out_ref):
    count = parts_ref.shape[0]
    rows = count * RQ
    row = iota((rows, rows), 0)
    column = iota((rows, rows), 1)
    slot, keep = row // KB, row % KB
    from_row = keep % count * RQ + slot
    whole = (column == from_row + keep // count * (RQ // 2)).astype(F32).astype(BF16)
    tail = (column == from_row).astype(F32).astype(BF16)

    def group(g):
        return parts_ref[:, RQ + RQ * g : 2 * RQ + RQ * g, :].reshape(rows, 128)

    for c in range(LAT // 128):
        block = mm(whole, group(c)).astype(BF16)
        for j in range(RQ // 2):
            out_ref[j, :, 128 * c : 128 * c + 128] = block[KB * j : KB * j + KB, :]
    block = mm(tail, group(4))
    upper = iota(block.shape, 0) % KB < count
    block = jnp.where(upper, block, pltpu.roll(block, ROPE, 1))[:, :ROPE].astype(BF16)
    for j in range(RQ // 2):
        out_ref[j, :, LAT:] = block[KB * j : KB * j + KB, :]


def norm_kernel(parts_ref, gain_ref, out_ref, norm_ref):
    pairs = []
    squares = jnp.zeros((RQ, 128), F32)
    for j in range(H):
        pair = parts_ref[2 * j, :RQ, :].astype(F32) + parts_ref[2 * j + 1, :RQ, :].astype(F32)
        squares = squares + pair * pair
        pairs.append(pair)
    mean_sq = jnp.sum(squares, axis=1, keepdims=True) / WIDE
    norm_ref[...] = jnp.broadcast_to(jnp.sqrt(mean_sq), norm_ref.shape)
    inverse = lax.rsqrt(mean_sq + 1e-06)
    for j in range(H):
        cut = slice(j * 128, (j + 1) * 128)
        normed = (pairs[j] * inverse * gain_ref[:, cut].astype(F32)).astype(BF16)
        for d in range(out_ref.shape[0]):
            out_ref[d, :, cut] = normed


def top_kernel(rows_ref, head_ref, low_ref, high_ref, out_ref):
    rows = rows_ref[...].reshape(rows_ref.shape[0] * RQ, WIDE)
    logits = mm_nt(rows, head_ref[...])
    column = iota(logits.shape, 1)
    allowed = (column >= low_ref[...]) & (column < high_ref[...])
    best = jnp.max(jnp.where(allowed, logits, NEGATIVE), axis=1, keepdims=True)
    spread = jnp.where(
        iota((rows.shape[0], 128), 1) == iota((rows.shape[0], 128), 0) % RQ, best, NEGATIVE
    )
    spread = jnp.max(spread.reshape(rows_ref.shape[0], RQ, 128), axis=1)
    for d in range(out_ref.shape[0]):
        out_ref[d] = spread


def body(
    hidden_in,
    query_weight,
    key_absorb,
    value_up,
    out_weight,
    latent_cache,
    cache_lengths,
    keep_lists,
    drop_weights,
    pack_dest,
    final_gain,
    head_weight,
    tenant_ranges,
    tenant_ids,
):
    seq_count = lax.axis_size("sx") * lax.axis_size("sz")
    mp_count = lax.axis_size("y") * lax.axis_size("c")
    seq_index = lax.axis_index(SEQ)
    mp_index = lax.axis_index(MP)
    slot_count = RQ // 2

    query_part = mm(hidden_in, query_weight).astype(BF16)
    query_part = jnp.pad(query_part, ((0, 0), (0, 128 - HALF)))
    query_part = jnp.where(seq_index % 2 == 0, query_part, jnp.roll(query_part, HALF, axis=1))
    query_all = lax.all_to_all(
        jnp.broadcast_to(query_part[None], (seq_count, RQ, 128)), SEQ, 0, 0, tiled=True
    )

    positions = jnp.arange(BLK, dtype=jnp.int32)
    keep_onehot = keep_lists[:, 0, :, None] == positions[None, None, :]
    kept_flag = jnp.sum(keep_onehot.astype(jnp.int32), axis=1)
    weights_dropped = (drop_weights * (1 - kept_flag)).astype(BF16)
    live_here = cache_lengths > seq_index * BLK
    mass = jnp.sum(weights_dropped.astype(F32), axis=1)
    summed = jnp.einsum("nt,ntc->nc", weights_dropped, latent_cache, preferred_element_type=F32)
    summary = (summed / mass[:, None]).astype(BF16)
    dest_here = lax.dynamic_slice_in_dim(pack_dest, seq_index, 1, 1)[:, 0]
    owners = jnp.arange(seq_count, dtype=jnp.int32)
    send_onehot = (dest_here[None, :] // slot_count == owners[:, None]) & (dest_here[None, :] >= 0)
    summ_send = mm(send_onehot.astype(BF16), summary).astype(BF16)
    summ_send = jnp.pad(summ_send.reshape(seq_count, RQ, ROW // RQ), ((0, 0), (0, 0), (0, 128 - ROW // RQ)))

    cache_t = jnp.swapaxes(latent_cache, 1, 2)
    keep_cols = keep_lists[:, 0, :].reshape(RQ, 2, seq_count).transpose(2, 0, 1)
    message = vmem_call(
        spread_kernel,
        pltpu.HBM((seq_count, 80, 128), BF16),
        [pltpu.VMEM((seq_count, 72, 128), BF16), pltpu.SemaphoreType.DMA],
        out_specs=APART,
    )(cache_t, keep_cols.reshape(seq_count * RQ, 2))

    live_f = jnp.broadcast_to(live_here.astype(F32)[:, None], (RQ, BLK))
    mask_f = live_f * kept_flag.astype(F32)
    part = vmem_call(
        attend_kernel,
        pltpu.HBM((seq_count, 40, 128), BF16),
        [
            pltpu.VMEM((H * RQ, LAT), F32),
            pltpu.VMEM((H * RQ, ROPE), F32),
            pltpu.VMEM(key_absorb.shape, BF16),
            pltpu.SemaphoreType.DMA((H,)),
        ],
        in_specs=[WHOLE, APART] + [WHOLE] * 6,
    )(
        query_all,
        key_absorb,
        cache_t,
        summary[:, :LAT],
        summary[:, LAT:],
        mask_f,
        live_f,
        summ_send,
    )
    part = lax.all_to_all(part, SEQ, 0, 0, tiled=True)

    half = (jnp.arange(RQ) // (RQ // 2) == seq_index % 2).astype(F32)
    message = vmem_call(
        merge_kernel,
        pltpu.HBM((seq_count, 80, 128), BF16),
        [
            pltpu.VMEM((seq_count, RQ, 128), BF16),
            pltpu.VMEM((LAT, VH), BF16),
            pltpu.SemaphoreType.DMA((2,)),
        ],
        in_specs=[SCALAR, WHOLE, APART, WHOLE, APART],
        out_specs=APART,
        input_output_aliases={4: 0},
    )(
        (seq_index // 2)[None],
        part,
        value_up,
        jnp.broadcast_to(half[:, None], (RQ, 128)),
        message,
    )
    values = lax.all_to_all(message, SEQ, 0, 0, tiled=True)
    slots = seq_index * slot_count + jnp.arange(slot_count, dtype=jnp.int32)
    summ_pick = jnp.any(pack_dest[None, :, :] == slots[:, None, None], axis=1)
    packed_summary = jnp.einsum(
        "js,sab->jab",
        summ_pick.astype(BF16),
        part[:, 32:40, : ROW // RQ],
        preferred_element_type=F32,
    )
    packed_summary = packed_summary.astype(BF16).reshape(slot_count, ROW)

    col_width = out_weight.shape[1]
    residual = lax.dynamic_slice_in_dim(hidden_in, seq_index * col_width, col_width, 1)
    out_t = out_weight.T
    side = (jnp.arange(2 * col_width) // col_width == seq_index % 2).astype(F32)
    hidden_send, own = vmem_call(
        hidden_kernel,
        (
            pltpu.HBM((seq_count, 48, 128), BF16),
            jax.ShapeDtypeStruct((RQ, 2 * col_width), BF16),
        ),
    )(
        values,
        jnp.concatenate([out_t, out_t], axis=0),
        jnp.concatenate([residual, residual], axis=1),
        jnp.broadcast_to(side[None, :], (RQ, 2 * col_width)),
        pack_dest.T.reshape(1, -1),
    )
    hidden_out = own[:, :col_width]
    hidden_all = lax.all_to_all(hidden_send, SEQ, 0, 0, tiled=True)
    packed_rows = vmem_call(settle_kernel, jax.ShapeDtypeStruct((slot_count, KB, ROW), BF16))(
        hidden_all
    )
    normed, norms = vmem_call(
        norm_kernel,
        (
            pltpu.HBM((mp_count, RQ, WIDE), BF16),
            jax.ShapeDtypeStruct((RQ, 128), F32),
        ),
    )(hidden_all, final_gain[None, :])
    state_norm = norms[:, 0]
    normed = lax.all_to_all(normed, MP, 0, 0, tiled=True)

    vocab_width = head_weight.shape[1]
    start = (seq_index * mp_count + mp_index) * vocab_width
    tenant_onehot = (tenant_ids[:, None] == jnp.arange(TENANTS, dtype=jnp.int32)[None, :]).astype(
        jnp.int32
    )
    window_low = jnp.sum(tenant_onehot * tenant_ranges[None, :, 0], axis=1) - start
    window_high = jnp.sum(tenant_onehot * tenant_ranges[None, :, 1], axis=1) - start
    best = vmem_call(top_kernel, pltpu.HBM((seq_count, mp_count, 128), F32))(
        normed, head_weight.T, window_low[:, None], window_high[:, None]
    )
    best = lax.all_to_all(best.reshape(seq_count * mp_count, 1, 128), ALL, 0, 0, tiled=True)
    top_logit = jnp.max(best[:, 0, :], axis=0)[:RQ]
    return (packed_rows, packed_summary, hidden_out, state_norm, top_logit)


def solution(mesh):
    seq_count, mp_count = mesh.devices.shape
    split = Mesh(
        mesh.devices.reshape(4, seq_count // 4, mp_count // 2, 2), ("sx", "sz", "y", "c")
    )
    in_specs = (
        P(MP, None),
        P(None, SEQ),
        P(),
        P(),
        P(None, SEQ),
        P(MP, SEQ, None),
        P(MP),
        P(MP, SEQ, None),
        P(MP, SEQ),
        P(MP, None),
        P(),
        P(None, ALL),
        P(),
        P(),
    )
    out_specs = (
        P(ALL, None, None),
        P(ALL, None),
        P(MP, SEQ),
        P(MP),
        P(MP),
    )
    return jax.shard_map(body, mesh=split, in_specs=in_specs, out_specs=out_specs, check_vma=False)
```

```python
import functools

import jax
import jax.numpy as jnp
from jax import lax
from jax.experimental import pallas as pl
from jax.experimental.pallas import tpu as pltpu
from jax.sharding import Mesh, PartitionSpec as P

H = 16
NOPE = 128
ROPE = 64
LAT = 512
VH = 128
BLK = 128
KB = 64
TENANTS = 4
RQ = 8
ROW = LAT + ROPE
HALF = (NOPE + ROPE) // 2
WIDE = H * VH
SEQ = ("sx", "sz")
MP = ("y", "c")
ALL = SEQ + MP

NEGATIVE = -1e30
F32 = jnp.float32
BF16 = jnp.bfloat16
NT = (((1,), (1,)), ((), ()))


def mm(a, b):
    return jnp.dot(a, b, preferred_element_type=F32)


def mm_nt(a, b):
    return lax.dot_general(a, b, NT, preferred_element_type=F32)


def iota(shape, axis):
    return lax.broadcasted_iota(jnp.int32, shape, axis)


WHOLE = pl.BlockSpec(memory_space=pltpu.VMEM)
APART = pl.BlockSpec(memory_space=pltpu.HBM)
SCALAR = pl.BlockSpec(memory_space=pltpu.SMEM)


def vmem_call(kernel, out_shape, scratch=(), limit=16 << 20, **specs):
    return pl.pallas_call(
        kernel,
        out_shape=out_shape,
        scratch_shapes=list(scratch),
        **specs,
        compiler_params=pltpu.CompilerParams(vmem_limit_bytes=limit),
    )


def in_parts(x):
    high = x.astype(BF16).astype(F32)
    rest = x - high
    middle = rest.astype(BF16).astype(F32)
    return (high, middle, rest - middle)


def query_kernel(side_ref, hidden_ref, weight_ref, out_ref, hidden_here, weight_here, sems):
    first = pltpu.make_async_copy(hidden_ref, hidden_here, sems.at[0])
    second = pltpu.make_async_copy(weight_ref, weight_here, sems.at[1])
    first.start()
    second.start()
    first.wait()
    second.wait()
    query = mm_nt(hidden_here[...], weight_here[...]).astype(BF16).astype(F32)
    query = jnp.concatenate([query, jnp.zeros((RQ, 128 - HALF), F32)], axis=1)
    query = jnp.where(side_ref[0] == 0, query, pltpu.roll(query, HALF, 1)).astype(BF16)
    for d in range(out_ref.shape[0]):
        out_ref[d] = query


def spread_kernel(head_ref, cache_ref, keep_ref, up_ref, message_ref, up_here, out_ref, sems):
    fetch = pltpu.make_async_copy(up_ref.at[head_ref[0]], up_here, sems.at[1])
    fetch.start()
    rows = out_ref.shape[0] * RQ
    lane = iota((rows, BLK), 1)
    request = iota((rows, BLK), 0) % RQ
    keys = keep_ref[...]
    none = jnp.zeros((ROPE, BLK), BF16)
    tail = jnp.zeros((rows, 2 * ROPE), F32)
    for k in range(2):
        kept = jnp.zeros((rows, LAT), F32)
        chosen = jnp.where(lane == keys[:, k : k + 1], request, -1)
        for r in range(RQ):
            onehot = (chosen == r).astype(F32).astype(BF16)
            kept = kept + mm_nt(onehot, cache_ref[r, :LAT, :])
            rope = cache_ref[r, LAT:, :]
            rope = jnp.concatenate([rope, none] if k == 0 else [none, rope], axis=0)
            tail = tail + mm_nt(onehot, rope)
        for c in range(LAT // 128):
            at = (2 * c + k) * RQ
            for i in range(out_ref.shape[0]):
                out_ref[i, at : at + RQ, :] = kept[
                    RQ * i : RQ * i + RQ, 128 * c : 128 * c + 128
                ].astype(BF16)
    for i in range(out_ref.shape[0]):
        out_ref[i, 64:72, :] = tail[RQ * i : RQ * i + RQ, :].astype(BF16)
    copy = pltpu.make_async_copy(out_ref, message_ref.at[:, RQ:, :], sems.at[0])
    copy.start()
    copy.wait()
    fetch.wait()


def attend_kernel(
    query_ref,
    absorb_ref,
    cache_ref,
    summ_ref,
    summ_tail_ref,
    mask_ref,
    live_ref,
    summ_send_ref,
    out_ref,
    lat_ref,
    tail_ref,
    absorb_here,
    sems,
):
    parts = sems.shape[0]
    step = H // parts
    copies = []
    for k in range(parts):
        cut = slice(step * k, step * k + step)
        copies.append(pltpu.make_async_copy(absorb_ref.at[cut], absorb_here.at[cut], sems.at[k]))
    for copy in copies:
        copy.start()
    for h in range(H):
        if h % step == 0:
            copies[h // step].wait()
        first = query_ref[2 * h].astype(F32)
        second = query_ref[2 * h + 1].astype(F32)
        nope = jnp.where(iota(first.shape, 1) < HALF, first, second).astype(BF16)
        lat_ref[8 * h : 8 * h + 8, :] = mm(nope, absorb_here[h])
        tail_ref[8 * h : 8 * h + 8, :] = second[:, :ROPE]
    lat = lat_ref[...].astype(BF16)
    tail = tail_ref[...].astype(BF16)
    rows = H * RQ
    request = iota((rows, BLK), 0) % RQ
    scores = jnp.zeros((rows, BLK), F32)
    for r in range(RQ):
        found = mm(lat, cache_ref[r, :LAT, :]) + mm(tail, cache_ref[r, LAT:, :])
        scores = jnp.where(request == r, found, scores)
    scale = (NOPE + ROPE) ** (-0.5)
    usable = jnp.concatenate([mask_ref[...]] * H, axis=0) > 0.0
    live = jnp.concatenate([live_ref[...]] * H, axis=0) > 0.0
    scores = jnp.where(usable, scores * scale, NEGATIVE)
    summ_all = mm_nt(lat, summ_ref[...]) + mm_nt(tail, summ_tail_ref[...])
    own = iota((rows, RQ), 1) == iota((rows, RQ), 0) % RQ
    summ = jnp.sum(jnp.where(own, summ_all, 0.0), axis=1, keepdims=True)
    summ = summ * scale + jnp.log(F32(BLK - KB))
    live_col = live[:, :1]
    summ = jnp.where(live_col, summ, NEGATIVE)
    top = jnp.maximum(jnp.max(scores, axis=1, keepdims=True), summ)
    weights = jnp.where(usable, jnp.exp(scores - top), 0.0)
    summ_weight = jnp.where(live_col, jnp.exp(summ - top), 0.0)
    total = jnp.sum(weights, axis=1, keepdims=True) + summ_weight
    summ_spread = jnp.where(own, summ_weight, 0.0)
    high = weights.astype(BF16)
    low = (weights - high.astype(F32)).astype(BF16)
    summ_high = summ_spread.astype(BF16)
    summ_low = (summ_spread - summ_high.astype(F32)).astype(BF16)
    weighted = mm(summ_high, summ_ref[...]) + mm(summ_low, summ_ref[...])
    none = jnp.zeros((rows, BLK), BF16)
    for r in range(RQ):
        keys = cache_ref[r, :LAT, :]
        weighted = weighted + mm_nt(jnp.where(request == r, high, none), keys)
        weighted = weighted + mm_nt(jnp.where(request == r, low, none), keys)

    def halves(first, second):
        upper = iota(first.shape, 0) % RQ < RQ // 2
        return (
            jnp.where(upper, first, pltpu.roll(second, RQ // 2, 0)),
            jnp.where(upper, pltpu.roll(first, rows - RQ // 2, 0), second),
        )

    large = weighted.astype(BF16).astype(F32)
    sent = halves(large, weighted - large)
    lane = iota((rows, 128), 1)
    side = jnp.zeros((rows, 128), F32)
    for at, column in enumerate(in_parts(top) + in_parts(total)):
        side = jnp.where(lane == 96 + at, column, side)
    sides = halves(side, side)
    for h in range(H):
        cut = slice(RQ * h, RQ * h + RQ)
        for half in range(2):
            d = 2 * h + half
            for c in range(LAT // 128):
                out_ref[d, RQ * c : RQ * c + RQ, :] = sent[half][
                    cut, 128 * c : 128 * c + 128
                ].astype(BF16)
            out_ref[d, 32:40, :] = (sides[half][cut] + summ_send_ref[d].astype(F32)).astype(BF16)


def merge_kernel(parts_ref, up_ref, half_ref, before_ref, message_ref, out_ref, sem):
    count = parts_ref.shape[0]
    sides = []
    for i in range(count):
        side = parts_ref[i, 32:40, :].astype(F32)
        sides.append(side + pltpu.roll(side, 127, 1) + pltpu.roll(side, 126, 1))
    lane = iota((RQ, 128), 1)
    sides = [jnp.where((lane == 96) | (lane == 99), one, 0.0) for one in sides]
    top = functools.reduce(jnp.maximum, [one[:, 96:97] for one in sides])
    factors = [jnp.exp(one[:, 96:97] - top) for one in sides]
    total = functools.reduce(jnp.add, [f * one[:, 99:100] for f, one in zip(factors, sides)])
    attended = []
    for c in range(LAT // 128):
        column = jnp.zeros((RQ, 128), F32)
        for i in range(count):
            block = parts_ref[i, RQ * c : RQ * c + RQ, :].astype(F32)
            column = column + factors[i] * block
        column = column + pltpu.roll(column, RQ // 2, 0)
        attended.append((column / total).astype(BF16))
    values = mm(jnp.concatenate(attended, axis=1), up_ref[...])
    values = jnp.where(half_ref[...] > 0.0, values, 0.0).astype(BF16)
    for d in range(out_ref.shape[0]):
        out_ref[d] = values
    copy = pltpu.make_async_copy(out_ref, message_ref.at[:, :RQ, :], sem)
    copy.start()
    copy.wait()


def hidden_kernel(parts_ref, weight_ref, residual_ref, side_ref, dest_ref, out_ref, own_ref):
    count = parts_ref.shape[0]
    values = [
        (parts_ref[2 * h, :RQ, :].astype(F32) + parts_ref[2 * h + 1, :RQ, :].astype(F32)).astype(BF16)
        for h in range(H)
    ]
    total = mm_nt(jnp.concatenate(values, axis=1), weight_ref[...])
    total = residual_ref[...].astype(F32) + total
    own_ref[...] = total.astype(BF16)
    both = jnp.where(side_ref[...] > 0.0, total, 0.0).astype(BF16)
    for d in range(count):
        out_ref[d, :RQ, :] = both
    rows = count * RQ
    row = iota((rows, rows), 0)
    matches = dest_ref[...] == row // RQ * (RQ // 2) + row % (RQ // 2)
    upper = row % RQ < RQ // 2
    first = (matches & upper).astype(F32).astype(BF16)
    second = (matches & ~upper).astype(F32).astype(BF16)

    def group(g):
        return parts_ref[:, RQ + RQ * g : 2 * RQ + RQ * g, :].reshape(rows, 128)

    for q in range(5):
        picked = mm(first, group(2 * q))
        if q < 4:
            picked = picked + mm(second, group(2 * q + 1))
        out_ref[:, RQ + RQ * q : 2 * RQ + RQ * q, :] = picked.astype(BF16).reshape(count, RQ, 128)


def settle_kernel(parts_ref, out_ref):
    count = parts_ref.shape[0]
    rows = count * RQ
    row = iota((rows, rows), 0)
    column = iota((rows, rows), 1)
    slot, keep = row // KB, row % KB
    from_row = keep % count * RQ + slot
    whole = (column == from_row + keep // count * (RQ // 2)).astype(F32).astype(BF16)
    tail = (column == from_row).astype(F32).astype(BF16)

    def group(g):
        return parts_ref[:, RQ + RQ * g : 2 * RQ + RQ * g, :].reshape(rows, 128)

    for c in range(LAT // 128):
        block = mm(whole, group(c)).astype(BF16)
        for j in range(RQ // 2):
            out_ref[j, :, 128 * c : 128 * c + 128] = block[KB * j : KB * j + KB, :]
    block = mm(tail, group(4))
    upper = iota(block.shape, 0) % KB < count
    block = jnp.where(upper, block, pltpu.roll(block, ROPE, 1))[:, :ROPE].astype(BF16)
    for j in range(RQ // 2):
        out_ref[j, :, LAT:] = block[KB * j : KB * j + KB, :]


def norm_kernel(parts_ref, gain_ref, out_ref, norm_ref):
    pairs = []
    squares = jnp.zeros((RQ, 128), F32)
    for j in range(H):
        pair = parts_ref[2 * j, :RQ, :].astype(F32) + parts_ref[2 * j + 1, :RQ, :].astype(F32)
        squares = squares + pair * pair
        pairs.append(pair)
    mean_sq = jnp.sum(squares, axis=1, keepdims=True) / WIDE
    norm_ref[...] = jnp.broadcast_to(jnp.sqrt(mean_sq), norm_ref.shape)
    inverse = lax.rsqrt(mean_sq + 1e-06)
    for j in range(H):
        cut = slice(j * 128, (j + 1) * 128)
        normed = (pairs[j] * inverse * gain_ref[:, cut].astype(F32)).astype(BF16)
        for d in range(out_ref.shape[0]):
            out_ref[d, :, cut] = normed


def top_kernel(rows_ref, head_ref, low_ref, high_ref, out_ref):
    rows = rows_ref[...].reshape(rows_ref.shape[0] * RQ, WIDE)
    logits = mm_nt(rows, head_ref[...])
    column = iota(logits.shape, 1)
    allowed = (column >= low_ref[...]) & (column < high_ref[...])
    best = jnp.max(jnp.where(allowed, logits, NEGATIVE), axis=1, keepdims=True)
    spread = jnp.where(
        iota((rows.shape[0], 128), 1) == iota((rows.shape[0], 128), 0) % RQ, best, NEGATIVE
    )
    spread = jnp.max(spread.reshape(rows_ref.shape[0], RQ, 128), axis=1)
    for d in range(out_ref.shape[0]):
        out_ref[d] = spread


def body(
    hidden_in,
    query_weight,
    key_absorb,
    value_up,
    out_weight,
    latent_cache,
    cache_lengths,
    keep_lists,
    drop_weights,
    pack_dest,
    final_gain,
    head_weight,
    tenant_ranges,
    tenant_ids,
):
    seq_count = lax.axis_size("sx") * lax.axis_size("sz")
    mp_count = lax.axis_size("y") * lax.axis_size("c")
    seq_index = lax.axis_index(SEQ)
    mp_index = lax.axis_index(MP)
    slot_count = RQ // 2

    query_send = vmem_call(
        query_kernel,
        pltpu.HBM((seq_count, RQ, 128), BF16),
        [
            pltpu.VMEM(hidden_in.shape, BF16),
            pltpu.VMEM(query_weight.shape[::-1], BF16),
            pltpu.SemaphoreType.DMA((2,)),
        ],
        in_specs=[SCALAR, APART, APART],
    )(
        (seq_index % 2)[None],
        pltpu.with_memory_space_constraint(hidden_in, pltpu.HBM),
        pltpu.with_memory_space_constraint(query_weight.T, pltpu.HBM),
    )
    query_all = lax.all_to_all(query_send, SEQ, 0, 0, tiled=True)

    positions = jnp.arange(BLK, dtype=jnp.int32)
    keep_onehot = keep_lists[:, 0, :, None] == positions[None, None, :]
    kept_flag = jnp.sum(keep_onehot.astype(jnp.int32), axis=1)
    weights_dropped = (drop_weights * (1 - kept_flag)).astype(BF16)
    live_here = cache_lengths > seq_index * BLK
    mass = jnp.sum(weights_dropped.astype(F32), axis=1)
    summed = jnp.einsum("nt,ntc->nc", weights_dropped, latent_cache, preferred_element_type=F32)
    summary = (summed / mass[:, None]).astype(BF16)
    dest_here = lax.dynamic_slice_in_dim(pack_dest, seq_index, 1, 1)[:, 0]
    owners = jnp.arange(seq_count, dtype=jnp.int32)
    send_onehot = (dest_here[None, :] // slot_count == owners[:, None]) & (dest_here[None, :] >= 0)
    summ_send = mm(send_onehot.astype(BF16), summary).astype(BF16)
    summ_send = jnp.pad(summ_send.reshape(seq_count, RQ, ROW // RQ), ((0, 0), (0, 0), (0, 128 - ROW // RQ)))

    cache_t = jnp.swapaxes(latent_cache, 1, 2)
    keep_cols = keep_lists[:, 0, :].reshape(RQ, 2, seq_count).transpose(2, 0, 1)
    message, up_here = vmem_call(
        spread_kernel,
        (pltpu.HBM((seq_count, 80, 128), BF16), pltpu.VMEM((LAT, VH), BF16)),
        [pltpu.VMEM((seq_count, 72, 128), BF16), pltpu.SemaphoreType.DMA((2,))],
        in_specs=[SCALAR, WHOLE, WHOLE, APART],
        out_specs=(APART, WHOLE),
    )(
        (seq_index // 2)[None],
        cache_t,
        keep_cols.reshape(seq_count * RQ, 2),
        pltpu.with_memory_space_constraint(value_up, pltpu.HBM),
    )

    live_f = jnp.broadcast_to(live_here.astype(F32)[:, None], (RQ, BLK))
    mask_f = live_f * kept_flag.astype(F32)
    part = vmem_call(
        attend_kernel,
        pltpu.HBM((seq_count, 40, 128), BF16),
        [
            pltpu.VMEM((H * RQ, LAT), F32),
            pltpu.VMEM((H * RQ, ROPE), F32),
            pltpu.VMEM(key_absorb.shape, BF16),
            pltpu.SemaphoreType.DMA((4,)),
        ],
        in_specs=[WHOLE, APART] + [WHOLE] * 6,
    )(
        query_all,
        pltpu.with_memory_space_constraint(key_absorb, pltpu.HBM),
        cache_t,
        summary[:, :LAT],
        summary[:, LAT:],
        mask_f,
        live_f,
        summ_send,
    )
    part = lax.all_to_all(part, SEQ, 0, 0, tiled=True)

    half = (jnp.arange(RQ) // (RQ // 2) == seq_index % 2).astype(F32)
    message = vmem_call(
        merge_kernel,
        pltpu.HBM((seq_count, 80, 128), BF16),
        [
            pltpu.VMEM((seq_count, RQ, 128), BF16),
            pltpu.SemaphoreType.DMA,
        ],
        in_specs=[WHOLE, WHOLE, WHOLE, APART],
        out_specs=APART,
        input_output_aliases={3: 0},
    )(
        part,
        pltpu.with_memory_space_constraint(up_here, pltpu.VMEM),
        jnp.broadcast_to(half[:, None], (RQ, 128)),
        message,
    )
    values = lax.all_to_all(message, SEQ, 0, 0, tiled=True)
    slots = seq_index * slot_count + jnp.arange(slot_count, dtype=jnp.int32)
    summ_pick = jnp.any(pack_dest[None, :, :] == slots[:, None, None], axis=1)
    packed_summary = jnp.einsum(
        "js,sab->jab",
        summ_pick.astype(BF16),
        part[:, 32:40, : ROW // RQ],
        preferred_element_type=F32,
    )
    packed_summary = packed_summary.astype(BF16).reshape(slot_count, ROW)

    col_width = out_weight.shape[1]
    residual = lax.dynamic_slice_in_dim(hidden_in, seq_index * col_width, col_width, 1)
    out_t = out_weight.T
    side = (jnp.arange(2 * col_width) // col_width == seq_index % 2).astype(F32)
    hidden_send, own = vmem_call(
        hidden_kernel,
        (
            pltpu.HBM((seq_count, 48, 128), BF16),
            jax.ShapeDtypeStruct((RQ, 2 * col_width), BF16),
        ),
    )(
        values,
        jnp.concatenate([out_t, out_t], axis=0),
        jnp.concatenate([residual, residual], axis=1),
        jnp.broadcast_to(side[None, :], (RQ, 2 * col_width)),
        pack_dest.T.reshape(1, -1),
    )
    hidden_out = own[:, :col_width]
    hidden_all = lax.all_to_all(hidden_send, SEQ, 0, 0, tiled=True)
    packed_rows = vmem_call(settle_kernel, jax.ShapeDtypeStruct((slot_count, KB, ROW), BF16))(
        hidden_all
    )
    normed, norms = vmem_call(
        norm_kernel,
        (
            pltpu.HBM((mp_count, RQ, WIDE), BF16),
            jax.ShapeDtypeStruct((RQ, 128), F32),
        ),
    )(hidden_all, final_gain[None, :])
    state_norm = norms[:, 0]
    normed = lax.all_to_all(normed, MP, 0, 0, tiled=True)

    vocab_width = head_weight.shape[1]
    start = (seq_index * mp_count + mp_index) * vocab_width
    tenant_onehot = (tenant_ids[:, None] == jnp.arange(TENANTS, dtype=jnp.int32)[None, :]).astype(
        jnp.int32
    )
    window_low = jnp.sum(tenant_onehot * tenant_ranges[None, :, 0], axis=1) - start
    window_high = jnp.sum(tenant_onehot * tenant_ranges[None, :, 1], axis=1) - start
    best = vmem_call(top_kernel, pltpu.HBM((seq_count, mp_count, 128), F32))(
        normed, head_weight.T, window_low[:, None], window_high[:, None]
    )
    best = lax.all_to_all(best.reshape(seq_count * mp_count, 1, 128), ALL, 0, 0, tiled=True)
    top_logit = jnp.max(best.reshape(seq_count, mp_count, 128), axis=(0, 1))[:RQ]
    return (packed_rows, packed_summary, hidden_out, state_norm, top_logit)


def solution(mesh):
    seq_count, mp_count = mesh.devices.shape
    split = Mesh(
        mesh.devices.reshape(4, seq_count // 4, mp_count // 2, 2), ("sx", "sz", "y", "c")
    )
    in_specs = (
        P(MP, None),
        P(None, SEQ),
        P(),
        P(),
        P(None, SEQ),
        P(MP, SEQ, None),
        P(MP),
        P(MP, SEQ, None),
        P(MP, SEQ),
        P(MP, None),
        P(),
        P(None, ALL),
        P(),
        P(),
    )
    out_specs = (
        P(ALL, None, None),
        P(ALL, None),
        P(MP, SEQ),
        P(MP),
        P(MP),
    )
    return jax.shard_map(body, mesh=split, in_specs=in_specs, out_specs=out_specs, check_vma=False)
```

```python
import functools

import jax
import jax.numpy as jnp
from jax import lax
from jax.experimental import pallas as pl
from jax.experimental.pallas import tpu as pltpu
from jax.sharding import Mesh, PartitionSpec as P

H = 16
NOPE = 128
ROPE = 64
LAT = 512
VH = 128
BLK = 128
KB = 64
TENANTS = 4
RQ = 8
ROW = LAT + ROPE
HALF = (NOPE + ROPE) // 2
WIDE = H * VH
SEQ = ("sx", "sz")
MP = ("y", "c")
ALL = SEQ + MP

NEGATIVE = -1e30
F32 = jnp.float32
BF16 = jnp.bfloat16
NT = (((1,), (1,)), ((), ()))


def mm(a, b):
    return jnp.dot(a, b, preferred_element_type=F32)


def mm_nt(a, b):
    return lax.dot_general(a, b, NT, preferred_element_type=F32)


def iota(shape, axis):
    return lax.broadcasted_iota(jnp.int32, shape, axis)


WHOLE = pl.BlockSpec(memory_space=pltpu.VMEM)
APART = pl.BlockSpec(memory_space=pltpu.HBM)
SCALAR = pl.BlockSpec(memory_space=pltpu.SMEM)


def vmem_call(kernel, out_shape, scratch=(), limit=16 << 20, **specs):
    return pl.pallas_call(
        kernel,
        out_shape=out_shape,
        scratch_shapes=list(scratch),
        **specs,
        compiler_params=pltpu.CompilerParams(vmem_limit_bytes=limit),
    )


def in_parts(x):
    high = x.astype(BF16).astype(F32)
    rest = x - high
    middle = rest.astype(BF16).astype(F32)
    return (high, middle, rest - middle)


def query_kernel(side_ref, hidden_ref, weight_ref, out_ref, hidden_here, weight_here, sems):
    first = pltpu.make_async_copy(hidden_ref, hidden_here, sems.at[0])
    second = pltpu.make_async_copy(weight_ref, weight_here, sems.at[1])
    first.start()
    second.start()
    first.wait()
    second.wait()
    query = mm_nt(hidden_here[...], weight_here[...]).astype(BF16).astype(F32)
    query = jnp.concatenate([query, jnp.zeros((RQ, 128 - HALF), F32)], axis=1)
    query = jnp.where(side_ref[0] == 0, query, pltpu.roll(query, HALF, 1)).astype(BF16)
    for d in range(out_ref.shape[0]):
        out_ref[d] = query


def spread_kernel(head_ref, cache_ref, keep_ref, up_ref, message_ref, up_here, out_ref, sems):
    fetch = pltpu.make_async_copy(up_ref.at[head_ref[0]], up_here, sems.at[1])
    fetch.start()
    rows = out_ref.shape[0] * RQ
    lane = iota((rows, BLK), 1)
    request = iota((rows, BLK), 0) % RQ
    keys = keep_ref[...]
    none = jnp.zeros((ROPE, BLK), BF16)
    tail = jnp.zeros((rows, 2 * ROPE), F32)
    for k in range(2):
        kept = jnp.zeros((rows, LAT), F32)
        chosen = jnp.where(lane == keys[:, k : k + 1], request, -1)
        for r in range(RQ):
            onehot = (chosen == r).astype(F32).astype(BF16)
            kept = kept + mm_nt(onehot, cache_ref[r, :LAT, :])
            rope = cache_ref[r, LAT:, :]
            rope = jnp.concatenate([rope, none] if k == 0 else [none, rope], axis=0)
            tail = tail + mm_nt(onehot, rope)
        for c in range(LAT // 128):
            at = (2 * c + k) * RQ
            for i in range(out_ref.shape[0]):
                out_ref[i, at : at + RQ, :] = kept[
                    RQ * i : RQ * i + RQ, 128 * c : 128 * c + 128
                ].astype(BF16)
    for i in range(out_ref.shape[0]):
        out_ref[i, 64:72, :] = tail[RQ * i : RQ * i + RQ, :].astype(BF16)
    copy = pltpu.make_async_copy(out_ref, message_ref.at[:, RQ:, :], sems.at[0])
    copy.start()
    copy.wait()
    fetch.wait()


def mask_kernel(kept_ref, live_ref, absorb_ref, out_ref):
    out_ref[...] = kept_ref[...] * live_ref[...]


def attend_kernel(
    query_ref,
    absorb_ref,
    cache_ref,
    summ_ref,
    summ_tail_ref,
    mask_ref,
    live_ref,
    summ_send_ref,
    out_ref,
    lat_ref,
    tail_ref,
):
    for h in range(H):
        first = query_ref[2 * h].astype(F32)
        second = query_ref[2 * h + 1].astype(F32)
        nope = jnp.where(iota(first.shape, 1) < HALF, first, second).astype(BF16)
        lat_ref[8 * h : 8 * h + 8, :] = mm(nope, absorb_ref[h])
        tail_ref[8 * h : 8 * h + 8, :] = second[:, :ROPE]
    lat = lat_ref[...].astype(BF16)
    tail = tail_ref[...].astype(BF16)
    rows = H * RQ
    request = iota((rows, BLK), 0) % RQ
    scores = jnp.zeros((rows, BLK), F32)
    for r in range(RQ):
        found = mm(lat, cache_ref[r, :LAT, :]) + mm(tail, cache_ref[r, LAT:, :])
        scores = jnp.where(request == r, found, scores)
    scale = (NOPE + ROPE) ** (-0.5)
    usable = jnp.concatenate([mask_ref[...]] * H, axis=0) > 0.0
    live = jnp.concatenate([live_ref[...]] * H, axis=0) > 0.0
    scores = jnp.where(usable, scores * scale, NEGATIVE)
    summ_all = mm_nt(lat, summ_ref[...]) + mm_nt(tail, summ_tail_ref[...])
    own = iota((rows, RQ), 1) == iota((rows, RQ), 0) % RQ
    summ = jnp.sum(jnp.where(own, summ_all, 0.0), axis=1, keepdims=True)
    summ = summ * scale + jnp.log(F32(BLK - KB))
    live_col = live[:, :1]
    summ = jnp.where(live_col, summ, NEGATIVE)
    top = jnp.maximum(jnp.max(scores, axis=1, keepdims=True), summ)
    weights = jnp.where(usable, jnp.exp(scores - top), 0.0)
    summ_weight = jnp.where(live_col, jnp.exp(summ - top), 0.0)
    total = jnp.sum(weights, axis=1, keepdims=True) + summ_weight
    summ_spread = jnp.where(own, summ_weight, 0.0)
    high = weights.astype(BF16)
    low = (weights - high.astype(F32)).astype(BF16)
    summ_high = summ_spread.astype(BF16)
    summ_low = (summ_spread - summ_high.astype(F32)).astype(BF16)
    weighted = mm(summ_high, summ_ref[...]) + mm(summ_low, summ_ref[...])
    none = jnp.zeros((rows, BLK), BF16)
    for r in range(RQ):
        keys = cache_ref[r, :LAT, :]
        weighted = weighted + mm_nt(jnp.where(request == r, high, none), keys)
        weighted = weighted + mm_nt(jnp.where(request == r, low, none), keys)

    def halves(first, second):
        upper = iota(first.shape, 0) % RQ < RQ // 2
        return (
            jnp.where(upper, first, pltpu.roll(second, RQ // 2, 0)),
            jnp.where(upper, pltpu.roll(first, rows - RQ // 2, 0), second),
        )

    large = weighted.astype(BF16).astype(F32)
    sent = halves(large, weighted - large)
    lane = iota((rows, 128), 1)
    side = jnp.zeros((rows, 128), F32)
    for at, column in enumerate(in_parts(top) + in_parts(total)):
        side = jnp.where(lane == 96 + at, column, side)
    sides = halves(side, side)
    for h in range(H):
        cut = slice(RQ * h, RQ * h + RQ)
        for half in range(2):
            d = 2 * h + half
            for c in range(LAT // 128):
                out_ref[d, RQ * c : RQ * c + RQ, :] = sent[half][
                    cut, 128 * c : 128 * c + 128
                ].astype(BF16)
            out_ref[d, 32:40, :] = (sides[half][cut] + summ_send_ref[d].astype(F32)).astype(BF16)


def merge_kernel(parts_ref, up_ref, half_ref, before_ref, message_ref, out_ref, sem):
    count = parts_ref.shape[0]
    sides = []
    for i in range(count):
        side = parts_ref[i, 32:40, :].astype(F32)
        sides.append(side + pltpu.roll(side, 127, 1) + pltpu.roll(side, 126, 1))
    lane = iota((RQ, 128), 1)
    sides = [jnp.where((lane == 96) | (lane == 99), one, 0.0) for one in sides]
    top = functools.reduce(jnp.maximum, [one[:, 96:97] for one in sides])
    factors = [jnp.exp(one[:, 96:97] - top) for one in sides]
    total = functools.reduce(jnp.add, [f * one[:, 99:100] for f, one in zip(factors, sides)])
    attended = []
    for c in range(LAT // 128):
        column = jnp.zeros((RQ, 128), F32)
        for i in range(count):
            block = parts_ref[i, RQ * c : RQ * c + RQ, :].astype(F32)
            column = column + factors[i] * block
        column = column + pltpu.roll(column, RQ // 2, 0)
        attended.append((column / total).astype(BF16))
    values = mm(jnp.concatenate(attended, axis=1), up_ref[...])
    values = jnp.where(half_ref[...] > 0.0, values, 0.0).astype(BF16)
    for d in range(out_ref.shape[0]):
        out_ref[d] = values
    copy = pltpu.make_async_copy(out_ref, message_ref.at[:, :RQ, :], sem)
    copy.start()
    copy.wait()


def hidden_kernel(parts_ref, weight_ref, residual_ref, side_ref, dest_ref, out_ref, own_ref):
    count = parts_ref.shape[0]
    values = [
        (parts_ref[2 * h, :RQ, :].astype(F32) + parts_ref[2 * h + 1, :RQ, :].astype(F32)).astype(BF16)
        for h in range(H)
    ]
    total = mm_nt(jnp.concatenate(values, axis=1), weight_ref[...])
    total = residual_ref[...].astype(F32) + total
    own_ref[...] = total.astype(BF16)
    both = jnp.where(side_ref[...] > 0.0, total, 0.0).astype(BF16)
    for d in range(count):
        out_ref[d, :RQ, :] = both
    rows = count * RQ
    row = iota((rows, rows), 0)
    matches = dest_ref[...] == row // RQ * (RQ // 2) + row % (RQ // 2)
    upper = row % RQ < RQ // 2
    first = (matches & upper).astype(F32).astype(BF16)
    second = (matches & ~upper).astype(F32).astype(BF16)

    def group(g):
        return parts_ref[:, RQ + RQ * g : 2 * RQ + RQ * g, :].reshape(rows, 128)

    for q in range(5):
        picked = mm(first, group(2 * q))
        if q < 4:
            picked = picked + mm(second, group(2 * q + 1))
        out_ref[:, RQ + RQ * q : 2 * RQ + RQ * q, :] = picked.astype(BF16).reshape(count, RQ, 128)


def settle_kernel(parts_ref, out_ref):
    count = parts_ref.shape[0]
    rows = count * RQ
    row = iota((rows, rows), 0)
    column = iota((rows, rows), 1)
    slot, keep = row // KB, row % KB
    from_row = keep % count * RQ + slot
    whole = (column == from_row + keep // count * (RQ // 2)).astype(F32).astype(BF16)
    tail = (column == from_row).astype(F32).astype(BF16)

    def group(g):
        return parts_ref[:, RQ + RQ * g : 2 * RQ + RQ * g, :].reshape(rows, 128)

    for c in range(LAT // 128):
        block = mm(whole, group(c)).astype(BF16)
        for j in range(RQ // 2):
            out_ref[j, :, 128 * c : 128 * c + 128] = block[KB * j : KB * j + KB, :]
    block = mm(tail, group(4))
    upper = iota(block.shape, 0) % KB < count
    block = jnp.where(upper, block, pltpu.roll(block, ROPE, 1))[:, :ROPE].astype(BF16)
    for j in range(RQ // 2):
        out_ref[j, :, LAT:] = block[KB * j : KB * j + KB, :]


def norm_kernel(parts_ref, gain_ref, out_ref, norm_ref):
    pairs = []
    squares = jnp.zeros((RQ, 128), F32)
    for j in range(H):
        pair = parts_ref[2 * j, :RQ, :].astype(F32) + parts_ref[2 * j + 1, :RQ, :].astype(F32)
        squares = squares + pair * pair
        pairs.append(pair)
    mean_sq = jnp.sum(squares, axis=1, keepdims=True) / WIDE
    norm_ref[...] = jnp.broadcast_to(jnp.sqrt(mean_sq), norm_ref.shape)
    inverse = lax.rsqrt(mean_sq + 1e-06)
    for j in range(H):
        cut = slice(j * 128, (j + 1) * 128)
        normed = (pairs[j] * inverse * gain_ref[:, cut].astype(F32)).astype(BF16)
        for d in range(out_ref.shape[0]):
            out_ref[d, :, cut] = normed


def top_kernel(rows_ref, head_ref, low_ref, high_ref, out_ref):
    rows = rows_ref[...].reshape(rows_ref.shape[0] * RQ, WIDE)
    logits = mm_nt(rows, head_ref[...])
    column = iota(logits.shape, 1)
    allowed = (column >= low_ref[...]) & (column < high_ref[...])
    best = jnp.max(jnp.where(allowed, logits, NEGATIVE), axis=1, keepdims=True)
    spread = jnp.where(
        iota((rows.shape[0], 128), 1) == iota((rows.shape[0], 128), 0) % RQ, best, NEGATIVE
    )
    spread = jnp.max(spread.reshape(rows_ref.shape[0], RQ, 128), axis=1)
    for d in range(out_ref.shape[0]):
        out_ref[d] = spread


def body(
    hidden_in,
    query_weight,
    key_absorb,
    value_up,
    out_weight,
    latent_cache,
    cache_lengths,
    keep_lists,
    drop_weights,
    pack_dest,
    final_gain,
    head_weight,
    tenant_ranges,
    tenant_ids,
):
    seq_count = lax.axis_size("sx") * lax.axis_size("sz")
    mp_count = lax.axis_size("y") * lax.axis_size("c")
    seq_index = lax.axis_index(SEQ)
    mp_index = lax.axis_index(MP)
    slot_count = RQ // 2

    query_send = vmem_call(
        query_kernel,
        pltpu.HBM((seq_count, RQ, 128), BF16),
        [
            pltpu.VMEM(hidden_in.shape, BF16),
            pltpu.VMEM(query_weight.shape[::-1], BF16),
            pltpu.SemaphoreType.DMA((2,)),
        ],
        in_specs=[SCALAR, APART, APART],
    )(
        (seq_index % 2)[None],
        pltpu.with_memory_space_constraint(hidden_in, pltpu.HBM),
        pltpu.with_memory_space_constraint(query_weight.T, pltpu.HBM),
    )
    query_all = lax.all_to_all(query_send, SEQ, 0, 0, tiled=True)

    positions = jnp.arange(BLK, dtype=jnp.int32)
    keep_onehot = keep_lists[:, 0, :, None] == positions[None, None, :]
    kept_flag = jnp.sum(keep_onehot.astype(jnp.int32), axis=1)
    weights_dropped = (drop_weights * (1 - kept_flag)).astype(BF16)
    live_here = cache_lengths > seq_index * BLK
    mass = jnp.sum(weights_dropped.astype(F32), axis=1)
    summed = jnp.einsum("nt,ntc->nc", weights_dropped, latent_cache, preferred_element_type=F32)
    summary = (summed / mass[:, None]).astype(BF16)
    dest_here = lax.dynamic_slice_in_dim(pack_dest, seq_index, 1, 1)[:, 0]
    owners = jnp.arange(seq_count, dtype=jnp.int32)
    send_onehot = (dest_here[None, :] // slot_count == owners[:, None]) & (dest_here[None, :] >= 0)
    summ_send = mm(send_onehot.astype(BF16), summary).astype(BF16)
    summ_send = jnp.pad(summ_send.reshape(seq_count, RQ, ROW // RQ), ((0, 0), (0, 0), (0, 128 - ROW // RQ)))

    cache_t = jnp.swapaxes(latent_cache, 1, 2)
    keep_cols = keep_lists[:, 0, :].reshape(RQ, 2, seq_count).transpose(2, 0, 1)
    message, up_here = vmem_call(
        spread_kernel,
        (pltpu.HBM((seq_count, 80, 128), BF16), pltpu.VMEM((LAT, VH), BF16)),
        [pltpu.VMEM((seq_count, 72, 128), BF16), pltpu.SemaphoreType.DMA((2,))],
        in_specs=[SCALAR, WHOLE, WHOLE, APART],
        out_specs=(APART, WHOLE),
    )(
        (seq_index // 2)[None],
        cache_t,
        keep_cols.reshape(seq_count * RQ, 2),
        pltpu.with_memory_space_constraint(value_up, pltpu.HBM),
    )

    live_f = jnp.broadcast_to(live_here.astype(F32)[:, None], (RQ, BLK))
    mask_f = vmem_call(mask_kernel, jax.ShapeDtypeStruct((RQ, BLK), F32))(
        kept_flag.astype(F32), live_f, key_absorb
    )
    part = vmem_call(
        attend_kernel,
        pltpu.HBM((seq_count, 40, 128), BF16),
        [
            pltpu.VMEM((H * RQ, LAT), F32),
            pltpu.VMEM((H * RQ, ROPE), F32),
        ],
    )(
        query_all,
        key_absorb,
        cache_t,
        summary[:, :LAT],
        summary[:, LAT:],
        mask_f,
        live_f,
        summ_send,
    )
    part = lax.all_to_all(part, SEQ, 0, 0, tiled=True)

    half = (jnp.arange(RQ) // (RQ // 2) == seq_index % 2).astype(F32)
    message = vmem_call(
        merge_kernel,
        pltpu.HBM((seq_count, 80, 128), BF16),
        [
            pltpu.VMEM((seq_count, RQ, 128), BF16),
            pltpu.SemaphoreType.DMA,
        ],
        in_specs=[WHOLE, WHOLE, WHOLE, APART],
        out_specs=APART,
        input_output_aliases={3: 0},
    )(
        part,
        pltpu.with_memory_space_constraint(up_here, pltpu.VMEM),
        jnp.broadcast_to(half[:, None], (RQ, 128)),
        message,
    )
    values = lax.all_to_all(message, SEQ, 0, 0, tiled=True)
    slots = seq_index * slot_count + jnp.arange(slot_count, dtype=jnp.int32)
    summ_pick = jnp.any(pack_dest[None, :, :] == slots[:, None, None], axis=1)
    packed_summary = jnp.einsum(
        "js,sab->jab",
        summ_pick.astype(BF16),
        part[:, 32:40, : ROW // RQ],
        preferred_element_type=F32,
    )
    packed_summary = packed_summary.astype(BF16).reshape(slot_count, ROW)

    col_width = out_weight.shape[1]
    residual = lax.dynamic_slice_in_dim(hidden_in, seq_index * col_width, col_width, 1)
    out_t = out_weight.T
    side = (jnp.arange(2 * col_width) // col_width == seq_index % 2).astype(F32)
    hidden_send, own = vmem_call(
        hidden_kernel,
        (
            pltpu.HBM((seq_count, 48, 128), BF16),
            jax.ShapeDtypeStruct((RQ, 2 * col_width), BF16),
        ),
    )(
        values,
        jnp.concatenate([out_t, out_t], axis=0),
        jnp.concatenate([residual, residual], axis=1),
        jnp.broadcast_to(side[None, :], (RQ, 2 * col_width)),
        pack_dest.T.reshape(1, -1),
    )
    hidden_out = own[:, :col_width]
    hidden_all = lax.all_to_all(hidden_send, SEQ, 0, 0, tiled=True)
    packed_rows = vmem_call(settle_kernel, jax.ShapeDtypeStruct((slot_count, KB, ROW), BF16))(
        hidden_all
    )
    normed, norms = vmem_call(
        norm_kernel,
        (
            pltpu.HBM((mp_count, RQ, WIDE), BF16),
            jax.ShapeDtypeStruct((RQ, 128), F32),
        ),
    )(hidden_all, final_gain[None, :])
    state_norm = norms[:, 0]
    normed = lax.all_to_all(normed, MP, 0, 0, tiled=True)

    vocab_width = head_weight.shape[1]
    start = (seq_index * mp_count + mp_index) * vocab_width
    tenant_onehot = (tenant_ids[:, None] == jnp.arange(TENANTS, dtype=jnp.int32)[None, :]).astype(
        jnp.int32
    )
    window_low = jnp.sum(tenant_onehot * tenant_ranges[None, :, 0], axis=1) - start
    window_high = jnp.sum(tenant_onehot * tenant_ranges[None, :, 1], axis=1) - start
    best = vmem_call(top_kernel, pltpu.HBM((seq_count, mp_count, 128), F32))(
        normed, head_weight.T, window_low[:, None], window_high[:, None]
    )
    best = lax.all_to_all(best.reshape(seq_count * mp_count, 1, 128), ALL, 0, 0, tiled=True)
    top_logit = jnp.max(best.reshape(seq_count, mp_count, 128), axis=(0, 1))[:RQ]
    return (packed_rows, packed_summary, hidden_out, state_norm, top_logit)


def solution(mesh):
    seq_count, mp_count = mesh.devices.shape
    split = Mesh(
        mesh.devices.reshape(4, seq_count // 4, mp_count // 2, 2), ("sx", "sz", "y", "c")
    )
    in_specs = (
        P(MP, None),
        P(None, SEQ),
        P(),
        P(),
        P(None, SEQ),
        P(MP, SEQ, None),
        P(MP),
        P(MP, SEQ, None),
        P(MP, SEQ),
        P(MP, None),
        P(),
        P(None, ALL),
        P(),
        P(),
    )
    out_specs = (
        P(ALL, None, None),
        P(ALL, None),
        P(MP, SEQ),
        P(MP),
        P(MP),
    )
    return jax.shard_map(body, mesh=split, in_specs=in_specs, out_specs=out_specs, check_vma=False)
```

```python
import functools

import jax
import jax.numpy as jnp
from jax import lax
from jax.experimental import pallas as pl
from jax.experimental.pallas import tpu as pltpu
from jax.sharding import Mesh, PartitionSpec as P

H = 16
NOPE = 128
ROPE = 64
LAT = 512
VH = 128
BLK = 128
KB = 64
TENANTS = 4
RQ = 8
ROW = LAT + ROPE
HALF = (NOPE + ROPE) // 2
WIDE = H * VH
SEQ = ("sx", "z1", "z0")
TURN = ("z0", "sx", "z1")
MP = ("y", "c")
ALL = SEQ + MP

NEGATIVE = -1e30
F32 = jnp.float32
BF16 = jnp.bfloat16
NT = (((1,), (1,)), ((), ()))


def mm(a, b):
    return jnp.dot(a, b, preferred_element_type=F32)


def mm_nt(a, b):
    return lax.dot_general(a, b, NT, preferred_element_type=F32)


def iota(shape, axis):
    return lax.broadcasted_iota(jnp.int32, shape, axis)


WHOLE = pl.BlockSpec(memory_space=pltpu.VMEM)
APART = pl.BlockSpec(memory_space=pltpu.HBM)
SCALAR = pl.BlockSpec(memory_space=pltpu.SMEM)


def turned(x, sizes):
    x = x.reshape(sizes + x.shape[1:])
    return jnp.moveaxis(x, 2, 0).reshape((-1,) + x.shape[3:])


def vmem_call(kernel, out_shape, scratch=(), limit=16 << 20, **specs):
    return pl.pallas_call(
        kernel,
        out_shape=out_shape,
        scratch_shapes=list(scratch),
        **specs,
        compiler_params=pltpu.CompilerParams(vmem_limit_bytes=limit),
    )


def in_parts(x):
    high = x.astype(BF16).astype(F32)
    rest = x - high
    middle = rest.astype(BF16).astype(F32)
    return (high, middle, rest - middle)


def query_kernel(side_ref, hidden_ref, weight_ref, out_ref, hidden_here, weight_here, sems):
    first = pltpu.make_async_copy(hidden_ref, hidden_here, sems.at[0])
    second = pltpu.make_async_copy(weight_ref, weight_here, sems.at[1])
    first.start()
    second.start()
    first.wait()
    second.wait()
    query = mm_nt(hidden_here[...], weight_here[...]).astype(BF16).astype(F32)
    query = jnp.concatenate([query, jnp.zeros((RQ, 128 - HALF), F32)], axis=1)
    query = jnp.where(side_ref[0] == 0, query, pltpu.roll(query, HALF, 1)).astype(BF16)
    for d in range(out_ref.shape[0]):
        out_ref[d] = query


def spread_kernel(head_ref, cache_ref, keep_ref, up_ref, message_ref, up_here, out_ref, sems):
    fetch = pltpu.make_async_copy(up_ref.at[head_ref[0]], up_here, sems.at[1])
    fetch.start()
    rows = out_ref.shape[0] * RQ
    lane = iota((rows, BLK), 1)
    request = iota((rows, BLK), 0) % RQ
    keys = keep_ref[...]
    none = jnp.zeros((ROPE, BLK), BF16)
    tail = jnp.zeros((rows, 2 * ROPE), F32)
    for k in range(2):
        kept = jnp.zeros((rows, LAT), F32)
        chosen = jnp.where(lane == keys[:, k : k + 1], request, -1)
        for r in range(RQ):
            onehot = (chosen == r).astype(F32).astype(BF16)
            kept = kept + mm_nt(onehot, cache_ref[r, :LAT, :])
            rope = cache_ref[r, LAT:, :]
            rope = jnp.concatenate([rope, none] if k == 0 else [none, rope], axis=0)
            tail = tail + mm_nt(onehot, rope)
        for c in range(LAT // 128):
            at = (2 * c + k) * RQ
            for i in range(out_ref.shape[0]):
                out_ref[i, at : at + RQ, :] = kept[
                    RQ * i : RQ * i + RQ, 128 * c : 128 * c + 128
                ].astype(BF16)
    for i in range(out_ref.shape[0]):
        out_ref[i, 64:72, :] = tail[RQ * i : RQ * i + RQ, :].astype(BF16)
    copy = pltpu.make_async_copy(out_ref, message_ref.at[:, RQ:, :], sems.at[0])
    copy.start()
    copy.wait()
    fetch.wait()


def mask_kernel(kept_ref, live_ref, absorb_ref, out_ref):
    out_ref[...] = kept_ref[...] * live_ref[...]


def attend_kernel(
    query_ref,
    absorb_ref,
    cache_ref,
    summ_ref,
    summ_tail_ref,
    mask_ref,
    live_ref,
    summ_send_ref,
    out_ref,
    lat_ref,
    tail_ref,
):
    for h in range(H):
        first = query_ref[2 * h].astype(F32)
        second = query_ref[2 * h + 1].astype(F32)
        nope = jnp.where(iota(first.shape, 1) < HALF, first, second).astype(BF16)
        lat_ref[8 * h : 8 * h + 8, :] = mm(nope, absorb_ref[h])
        tail_ref[8 * h : 8 * h + 8, :] = second[:, :ROPE]
    lat = lat_ref[...].astype(BF16)
    tail = tail_ref[...].astype(BF16)
    rows = H * RQ
    request = iota((rows, BLK), 0) % RQ
    scores = jnp.zeros((rows, BLK), F32)
    for r in range(RQ):
        found = mm(lat, cache_ref[r, :LAT, :]) + mm(tail, cache_ref[r, LAT:, :])
        scores = jnp.where(request == r, found, scores)
    scale = (NOPE + ROPE) ** (-0.5)
    usable = jnp.concatenate([mask_ref[...]] * H, axis=0) > 0.0
    live = jnp.concatenate([live_ref[...]] * H, axis=0) > 0.0
    scores = jnp.where(usable, scores * scale, NEGATIVE)
    summ_all = mm_nt(lat, summ_ref[...]) + mm_nt(tail, summ_tail_ref[...])
    own = iota((rows, RQ), 1) == iota((rows, RQ), 0) % RQ
    summ = jnp.sum(jnp.where(own, summ_all, 0.0), axis=1, keepdims=True)
    summ = summ * scale + jnp.log(F32(BLK - KB))
    live_col = live[:, :1]
    summ = jnp.where(live_col, summ, NEGATIVE)
    top = jnp.maximum(jnp.max(scores, axis=1, keepdims=True), summ)
    weights = jnp.where(usable, jnp.exp(scores - top), 0.0)
    summ_weight = jnp.where(live_col, jnp.exp(summ - top), 0.0)
    total = jnp.sum(weights, axis=1, keepdims=True) + summ_weight
    summ_spread = jnp.where(own, summ_weight, 0.0)
    high = weights.astype(BF16)
    low = (weights - high.astype(F32)).astype(BF16)
    summ_high = summ_spread.astype(BF16)
    summ_low = (summ_spread - summ_high.astype(F32)).astype(BF16)
    weighted = mm(summ_high, summ_ref[...]) + mm(summ_low, summ_ref[...])
    none = jnp.zeros((rows, BLK), BF16)
    for r in range(RQ):
        keys = cache_ref[r, :LAT, :]
        weighted = weighted + mm_nt(jnp.where(request == r, high, none), keys)
        weighted = weighted + mm_nt(jnp.where(request == r, low, none), keys)

    def halves(first, second):
        upper = iota(first.shape, 0) % RQ < RQ // 2
        return (
            jnp.where(upper, first, pltpu.roll(second, RQ // 2, 0)),
            jnp.where(upper, pltpu.roll(first, rows - RQ // 2, 0), second),
        )

    large = weighted.astype(BF16).astype(F32)
    sent = halves(large, weighted - large)
    lane = iota((rows, 128), 1)
    side = jnp.zeros((rows, 128), F32)
    for at, column in enumerate(in_parts(top) + in_parts(total)):
        side = jnp.where(lane == 96 + at, column, side)
    sides = halves(side, side)
    for h in range(H):
        cut = slice(RQ * h, RQ * h + RQ)
        for half in range(2):
            d = 2 * h + half
            for c in range(LAT // 128):
                out_ref[d, RQ * c : RQ * c + RQ, :] = sent[half][
                    cut, 128 * c : 128 * c + 128
                ].astype(BF16)
            out_ref[d, 32:40, :] = (sides[half][cut] + summ_send_ref[d].astype(F32)).astype(BF16)


def merge_kernel(parts_ref, up_ref, half_ref, before_ref, message_ref, out_ref, sem):
    count = parts_ref.shape[0]
    sides = []
    for i in range(count):
        side = parts_ref[i, 32:40, :].astype(F32)
        sides.append(side + pltpu.roll(side, 127, 1) + pltpu.roll(side, 126, 1))
    lane = iota((RQ, 128), 1)
    sides = [jnp.where((lane == 96) | (lane == 99), one, 0.0) for one in sides]
    top = functools.reduce(jnp.maximum, [one[:, 96:97] for one in sides])
    factors = [jnp.exp(one[:, 96:97] - top) for one in sides]
    total = functools.reduce(jnp.add, [f * one[:, 99:100] for f, one in zip(factors, sides)])
    attended = []
    for c in range(LAT // 128):
        column = jnp.zeros((RQ, 128), F32)
        for i in range(count):
            block = parts_ref[i, RQ * c : RQ * c + RQ, :].astype(F32)
            column = column + factors[i] * block
        column = column + pltpu.roll(column, RQ // 2, 0)
        attended.append((column / total).astype(BF16))
    values = mm(jnp.concatenate(attended, axis=1), up_ref[...])
    values = jnp.where(half_ref[...] > 0.0, values, 0.0).astype(BF16)
    for d in range(out_ref.shape[0]):
        out_ref[d] = values
    copy = pltpu.make_async_copy(out_ref, message_ref.at[:, :RQ, :], sem)
    copy.start()
    copy.wait()


def hidden_kernel(rank_of, parts_ref, weight_ref, residual_ref, side_ref, dest_ref, out_ref, own_ref):
    count = parts_ref.shape[0]
    values = [
        (
            parts_ref[rank_of[2 * h], :RQ, :].astype(F32)
            + parts_ref[rank_of[2 * h + 1], :RQ, :].astype(F32)
        ).astype(BF16)
        for h in range(H)
    ]
    total = mm_nt(jnp.concatenate(values, axis=1), weight_ref[...])
    total = residual_ref[...].astype(F32) + total
    own_ref[...] = total.astype(BF16)
    both = jnp.where(side_ref[...] > 0.0, total, 0.0).astype(BF16)
    for d in range(count):
        out_ref[d, :RQ, :] = both
    rows = count * RQ
    row = iota((rows, rows), 0)
    matches = dest_ref[...] == row // RQ * (RQ // 2) + row % (RQ // 2)
    upper = row % RQ < RQ // 2
    first = (matches & upper).astype(F32).astype(BF16)
    second = (matches & ~upper).astype(F32).astype(BF16)

    def group(g):
        return parts_ref[:, RQ + RQ * g : 2 * RQ + RQ * g, :].reshape(rows, 128)

    for q in range(5):
        picked = mm(first, group(2 * q))
        if q < 4:
            picked = picked + mm(second, group(2 * q + 1))
        out_ref[:, RQ + RQ * q : 2 * RQ + RQ * q, :] = picked.astype(BF16).reshape(count, RQ, 128)


def settle_kernel(inner, parts_ref, out_ref):
    count = parts_ref.shape[0]
    rows = count * RQ
    row = iota((rows, rows), 0)
    column = iota((rows, rows), 1)
    slot, keep = row // KB, row % KB
    rank = keep % count
    from_row = (rank % (count // inner) * inner + rank // (count // inner)) * RQ + slot
    whole = (column == from_row + keep // count * (RQ // 2)).astype(F32).astype(BF16)
    tail = (column == from_row).astype(F32).astype(BF16)

    def group(g):
        return parts_ref[:, RQ + RQ * g : 2 * RQ + RQ * g, :].reshape(rows, 128)

    for c in range(LAT // 128):
        block = mm(whole, group(c)).astype(BF16)
        for j in range(RQ // 2):
            out_ref[j, :, 128 * c : 128 * c + 128] = block[KB * j : KB * j + KB, :]
    block = mm(tail, group(4))
    upper = iota(block.shape, 0) % KB < count
    block = jnp.where(upper, block, pltpu.roll(block, ROPE, 1))[:, :ROPE].astype(BF16)
    for j in range(RQ // 2):
        out_ref[j, :, LAT:] = block[KB * j : KB * j + KB, :]


def norm_kernel(parts_ref, gain_ref, out_ref, norm_ref):
    pairs = []
    squares = jnp.zeros((RQ, 128), F32)
    for j in range(H):
        pair = parts_ref[2 * j, :RQ, :].astype(F32) + parts_ref[2 * j + 1, :RQ, :].astype(F32)
        squares = squares + pair * pair
        pairs.append(pair)
    mean_sq = jnp.sum(squares, axis=1, keepdims=True) / WIDE
    norm_ref[...] = jnp.broadcast_to(jnp.sqrt(mean_sq), norm_ref.shape)
    inverse = lax.rsqrt(mean_sq + 1e-06)
    for j in range(H):
        cut = slice(j * 128, (j + 1) * 128)
        normed = (pairs[j] * inverse * gain_ref[:, cut].astype(F32)).astype(BF16)
        for d in range(out_ref.shape[0]):
            out_ref[d, :, cut] = normed


def top_kernel(rows_ref, head_ref, low_ref, high_ref, out_ref):
    rows = rows_ref[...].reshape(rows_ref.shape[0] * RQ, WIDE)
    logits = mm_nt(rows, head_ref[...])
    column = iota(logits.shape, 1)
    allowed = (column >= low_ref[...]) & (column < high_ref[...])
    best = jnp.max(jnp.where(allowed, logits, NEGATIVE), axis=1, keepdims=True)
    spread = jnp.where(
        iota((rows.shape[0], 128), 1) == iota((rows.shape[0], 128), 0) % RQ, best, NEGATIVE
    )
    spread = jnp.max(spread.reshape(rows_ref.shape[0], RQ, 128), axis=1)
    for d in range(out_ref.shape[0]):
        out_ref[d] = spread


def body(
    hidden_in,
    query_weight,
    key_absorb,
    value_up,
    out_weight,
    latent_cache,
    cache_lengths,
    keep_lists,
    drop_weights,
    pack_dest,
    final_gain,
    head_weight,
    tenant_ranges,
    tenant_ids,
):
    sizes = (lax.axis_size("sx"), lax.axis_size("z1"), lax.axis_size("z0"))
    seq_count = sizes[0] * sizes[1] * sizes[2]
    rank_of = [s % sizes[2] * (seq_count // sizes[2]) + s // sizes[2] for s in range(seq_count)]
    mp_count = lax.axis_size("y") * lax.axis_size("c")
    seq_index = lax.axis_index(SEQ)
    mp_index = lax.axis_index(MP)
    slot_count = RQ // 2

    query_send = vmem_call(
        query_kernel,
        pltpu.HBM((seq_count, RQ, 128), BF16),
        [
            pltpu.VMEM(hidden_in.shape, BF16),
            pltpu.VMEM(query_weight.shape[::-1], BF16),
            pltpu.SemaphoreType.DMA((2,)),
        ],
        in_specs=[SCALAR, APART, APART],
    )(
        (seq_index % 2)[None],
        pltpu.with_memory_space_constraint(hidden_in, pltpu.HBM),
        pltpu.with_memory_space_constraint(query_weight.T, pltpu.HBM),
    )
    query_all = lax.all_to_all(query_send, SEQ, 0, 0, tiled=True)

    positions = jnp.arange(BLK, dtype=jnp.int32)
    keep_onehot = keep_lists[:, 0, :, None] == positions[None, None, :]
    kept_flag = jnp.sum(keep_onehot.astype(jnp.int32), axis=1)
    weights_dropped = (drop_weights * (1 - kept_flag)).astype(BF16)
    live_here = cache_lengths > seq_index * BLK
    mass = jnp.sum(weights_dropped.astype(F32), axis=1)
    summed = jnp.einsum("nt,ntc->nc", weights_dropped, latent_cache, preferred_element_type=F32)
    summary = (summed / mass[:, None]).astype(BF16)
    dest_here = lax.dynamic_slice_in_dim(pack_dest, seq_index, 1, 1)[:, 0]
    owners = jnp.arange(seq_count, dtype=jnp.int32)
    send_onehot = (dest_here[None, :] // slot_count == owners[:, None]) & (dest_here[None, :] >= 0)
    summ_send = mm(send_onehot.astype(BF16), summary).astype(BF16)
    summ_send = jnp.pad(summ_send.reshape(seq_count, RQ, ROW // RQ), ((0, 0), (0, 0), (0, 128 - ROW // RQ)))

    cache_t = jnp.swapaxes(latent_cache, 1, 2)
    keep_cols = keep_lists[:, 0, :].reshape(RQ, 2, seq_count).transpose(2, 0, 1)
    message, up_here = vmem_call(
        spread_kernel,
        (pltpu.HBM((seq_count, 80, 128), BF16), pltpu.VMEM((LAT, VH), BF16)),
        [pltpu.VMEM((seq_count, 72, 128), BF16), pltpu.SemaphoreType.DMA((2,))],
        in_specs=[SCALAR, WHOLE, WHOLE, APART],
        out_specs=(APART, WHOLE),
    )(
        (seq_index // 2)[None],
        cache_t,
        keep_cols.reshape(seq_count * RQ, 2),
        pltpu.with_memory_space_constraint(value_up, pltpu.HBM),
    )

    live_f = jnp.broadcast_to(live_here.astype(F32)[:, None], (RQ, BLK))
    mask_f = vmem_call(mask_kernel, jax.ShapeDtypeStruct((RQ, BLK), F32))(
        kept_flag.astype(F32), live_f, key_absorb
    )
    part = vmem_call(
        attend_kernel,
        pltpu.HBM((seq_count, 40, 128), BF16),
        [
            pltpu.VMEM((H * RQ, LAT), F32),
            pltpu.VMEM((H * RQ, ROPE), F32),
        ],
    )(
        query_all,
        key_absorb,
        cache_t,
        summary[:, :LAT],
        summary[:, LAT:],
        mask_f,
        live_f,
        summ_send,
    )
    part = lax.all_to_all(part, SEQ, 0, 0, tiled=True)

    half = (jnp.arange(RQ) // (RQ // 2) == seq_index % 2).astype(F32)
    message = vmem_call(
        merge_kernel,
        pltpu.HBM((seq_count, 80, 128), BF16),
        [
            pltpu.VMEM((seq_count, RQ, 128), BF16),
            pltpu.SemaphoreType.DMA,
        ],
        in_specs=[WHOLE, WHOLE, WHOLE, APART],
        out_specs=APART,
        input_output_aliases={3: 0},
    )(
        part,
        pltpu.with_memory_space_constraint(up_here, pltpu.VMEM),
        jnp.broadcast_to(half[:, None], (RQ, 128)),
        message,
    )
    values = lax.all_to_all(message, TURN, 0, 0, tiled=True)
    slots = seq_index * slot_count + jnp.arange(slot_count, dtype=jnp.int32)
    summ_pick = jnp.any(pack_dest[None, :, :] == slots[:, None, None], axis=1)
    packed_summary = jnp.einsum(
        "js,sab->jab",
        summ_pick.astype(BF16),
        part[:, 32:40, : ROW // RQ],
        preferred_element_type=F32,
    )
    packed_summary = packed_summary.astype(BF16).reshape(slot_count, ROW)

    col_width = out_weight.shape[1]
    residual = lax.dynamic_slice_in_dim(hidden_in, seq_index * col_width, col_width, 1)
    out_t = out_weight.T
    side = (jnp.arange(2 * col_width) // col_width == seq_index % 2).astype(F32)
    hidden_send, own = vmem_call(
        functools.partial(hidden_kernel, rank_of),
        (
            pltpu.HBM((seq_count, 48, 128), BF16),
            jax.ShapeDtypeStruct((RQ, 2 * col_width), BF16),
        ),
    )(
        values,
        jnp.concatenate([out_t, out_t], axis=0),
        jnp.concatenate([residual, residual], axis=1),
        jnp.broadcast_to(side[None, :], (RQ, 2 * col_width)),
        turned(pack_dest.T, sizes).reshape(1, -1),
    )
    hidden_out = own[:, :col_width]
    hidden_all = lax.all_to_all(hidden_send, SEQ, 0, 0, tiled=True)
    packed_rows = vmem_call(functools.partial(settle_kernel, sizes[2]), jax.ShapeDtypeStruct((slot_count, KB, ROW), BF16))(
        hidden_all
    )
    normed, norms = vmem_call(
        norm_kernel,
        (
            pltpu.HBM((mp_count, RQ, WIDE), BF16),
            jax.ShapeDtypeStruct((RQ, 128), F32),
        ),
    )(hidden_all, final_gain[None, :])
    state_norm = norms[:, 0]
    normed = lax.all_to_all(normed, MP, 0, 0, tiled=True)

    vocab_width = head_weight.shape[1]
    start = (seq_index * mp_count + mp_index) * vocab_width
    tenant_onehot = (tenant_ids[:, None] == jnp.arange(TENANTS, dtype=jnp.int32)[None, :]).astype(
        jnp.int32
    )
    window_low = jnp.sum(tenant_onehot * tenant_ranges[None, :, 0], axis=1) - start
    window_high = jnp.sum(tenant_onehot * tenant_ranges[None, :, 1], axis=1) - start
    best = vmem_call(top_kernel, pltpu.HBM((seq_count, mp_count, 128), F32))(
        normed, head_weight.T, window_low[:, None], window_high[:, None]
    )
    best = lax.all_to_all(best.reshape(seq_count * mp_count, 1, 128), ALL, 0, 0, tiled=True)
    top_logit = jnp.max(best.reshape(seq_count, mp_count, 128), axis=(0, 1))[:RQ]
    return (packed_rows, packed_summary, hidden_out, state_norm, top_logit)


def solution(mesh):
    seq_count, mp_count = mesh.devices.shape
    split = Mesh(
        mesh.devices.reshape(4, 2, seq_count // 8, mp_count // 2, 2), SEQ + MP
    )
    in_specs = (
        P(MP, None),
        P(None, SEQ),
        P(),
        P(),
        P(None, SEQ),
        P(MP, SEQ, None),
        P(MP),
        P(MP, SEQ, None),
        P(MP, SEQ),
        P(MP, None),
        P(),
        P(None, ALL),
        P(),
        P(),
    )
    out_specs = (
        P(ALL, None, None),
        P(ALL, None),
        P(MP, SEQ),
        P(MP),
        P(MP),
    )
    return jax.shard_map(body, mesh=split, in_specs=in_specs, out_specs=out_specs, check_vma=False)
```
